32 devices in a mesh: clips: 2 (over y), seq: 4 (over z), tp: 2 (over x), dp: 2 (over core).
Axes of the slice: x: 2, y: 2, z: 4, core: 2. Of those that a mesh axis runs over, the one named last changes fastest.
Arguments:
- video_query: bfloat16 [4, 512, 4096], P(('clips', 'dp'), 'seq', 'tp'), parts along dimension 0, may hold values from -384 to 384
- video_key: bfloat16 [4, 512, 4096], P(('clips', 'dp'), 'seq', 'tp'), parts along dimension 0, may hold values from -384 to 384
- video_value: bfloat16 [4, 512, 4096], P(('clips', 'dp'), 'seq', 'tp'), parts along dimension 0, may hold values from -6 to 6
- cross_query: bfloat16 [4, 512, 2048], P(('clips', 'dp'), 'seq', 'tp'), parts along dimension 0, may hold values from -384 to 384
- audio_key: bfloat16 [4, 32, 2048], P(('clips', 'dp'), 'seq', 'tp'), parts along dimension 0, may hold values from -384 to 384
- audio_value: bfloat16 [4, 32, 2048], P(('clips', 'dp'), 'seq', 'tp'), parts along dimension 0, may hold values from -6 to 6
- audio_query: bfloat16 [4, 32, 2048], P(('clips', 'dp'), 'seq', 'tp'), parts along dimension 0, may hold values from -384 to 384
- cross_key: bfloat16 [4, 512, 2048], P(('clips', 'dp'), 'seq', 'tp'), parts along dimension 0, may hold values from -384 to 384
- cross_value: bfloat16 [4, 512, 2048], P(('clips', 'dp'), 'seq', 'tp'), parts along dimension 0, may hold values from -6 to 6
- audio_input: bfloat16 [4, 32, 2048], P(('clips', 'dp'), 'seq'), parts along dimension 0, may hold values from -0.29882812 to 0.29882812
- norm_gain: float32 [2048], replicated, may hold values from 0.1 to 1.9
- up_weight: bfloat16 [2048, 8192], P('tp', 'seq'), may hold values from -0.125 to 0.125
- down_weight: bfloat16 [8192, 2048], P('seq', 'tp'), may hold values from -0.0625 to 0.0625
Outputs:
- video_mixed: bfloat16 [4, 512, 4096], P(('clips', 'dp'), 'seq', 'tp'), parts along dimension 0
- video_heard: bfloat16 [4, 512, 2048], P(('clips', 'dp'), 'seq', 'tp'), parts along dimension 0
- audio_seen: bfloat16 [4, 32, 2048], P(('clips', 'dp'), 'seq', 'tp'), parts along dimension 0
- audio_mlp: bfloat16 [4, 32, 2048], P(('clips', 'dp'), 'seq', 'tp'), parts along dimension 0
The draws below stay inside these ranges and needn't reach their ends.
There are 2 independent parts, one for each index of `clips`. The reference program is written for one: setup_inputs(seed, part) draws one part's arguments, and reference() takes and returns one part's arrays. A program takes and returns all parts, laid end to end along the dimension named above; an argument that names none is the same for every part. Nothing has to cross between parts.
All inputs are finite; a program needn't handle non-finite values.
Results may differ from the reference program's by a relative error of at most 0.013.
Values may be sent and summed in bfloat16 or wider, within the bound.
A program may use at most 64 MiB of HBM per device.

```python
import math
import jax
import jax.numpy as jnp
from jax import lax

VHEADS = 32
VHEAD = 128
CHEADS = 32
CHEAD = 64
FFA = 8192
BATCH = 2
VWIDTH = 4096
AUDIO_D = 2048
VIDEO_LEN = 512
AUDIO_LEN = 32


def make_pair(base_key, query_rows, key_rows, head_count, head_size):
    key_query, key_keys = jax.random.split(base_key, 2)
    queries = jnp.clip(jax.random.normal(key_query, (BATCH, query_rows, head_count, head_size), jnp.float32), -4.0, 4.0)
    keys_out = 2.0 * jnp.clip(jax.random.normal(key_keys, (BATCH, key_rows, head_count, head_size), jnp.float32), -4.0, 4.0)
    return (queries.reshape(BATCH, query_rows, head_count * head_size), keys_out.reshape(BATCH, key_rows, head_count * head_size))


def draw_video_query(key, part):
    return make_pair(jax.random.fold_in(key, 11), VIDEO_LEN, VIDEO_LEN, VHEADS, VHEAD)[0].astype(jnp.bfloat16)


def draw_video_key(key, part):
    return make_pair(jax.random.fold_in(key, 11), VIDEO_LEN, VIDEO_LEN, VHEADS, VHEAD)[1].astype(jnp.bfloat16)


def draw_cross_query(key, part):
    return make_pair(jax.random.fold_in(key, 12), VIDEO_LEN, AUDIO_LEN, CHEADS, CHEAD)[0].astype(jnp.bfloat16)


def draw_audio_key(key, part):
    return make_pair(jax.random.fold_in(key, 12), VIDEO_LEN, AUDIO_LEN, CHEADS, CHEAD)[1].astype(jnp.bfloat16)


def draw_audio_query(key, part):
    return make_pair(jax.random.fold_in(key, 13), AUDIO_LEN, VIDEO_LEN, CHEADS, CHEAD)[0].astype(jnp.bfloat16)


def draw_cross_key(key, part):
    return make_pair(jax.random.fold_in(key, 13), AUDIO_LEN, VIDEO_LEN, CHEADS, CHEAD)[1].astype(jnp.bfloat16)


def steps_of(key, shape, shards, least, largest):
    factor_of = 1.0
    for axis_at, shards_of in shards:
        steps = jax.random.uniform(jax.random.fold_in(jax.random.fold_in(key, 6), axis_at), (shards_of,), jnp.float32, least / len(shards), largest / len(shards))
        factor_of = factor_of * jnp.repeat(jnp.exp(steps), shape[axis_at] // shards_of).reshape((-1,) + (1,) * (len(shape) - 1 - axis_at))
    return factor_of


def bell_draw(rng, shape, spread, limit, shards=(), kind=jnp.bfloat16):
    factor_of = steps_of(rng, shape, shards, -0.22, 0.18) if shards else 1.0
    values = jax.random.normal(rng, shape, jnp.float32) * spread * factor_of
    return jnp.minimum(jnp.maximum(values, -limit), limit).astype(kind)


def setup_inputs(seed: int = 0, part: int = 0) -> dict:
    arg_keys = jax.random.split(jax.random.key(seed), 14)
    part_splits = jax.random.split(jax.random.fold_in(arg_keys[13], part), 14)
    video_query = draw_video_query(jax.random.fold_in(jax.random.fold_in(arg_keys[13], part), 71), part)
    video_key = draw_video_key(jax.random.fold_in(jax.random.fold_in(arg_keys[13], part), 71), part)
    video_value = bell_draw(part_splits[2], (BATCH, VIDEO_LEN, VWIDTH), 1.0, 6.0, ((0, 2), (1, 4), (2, 2)))
    cross_query = draw_cross_query(jax.random.fold_in(jax.random.fold_in(arg_keys[13], part), 71), part)
    audio_key = draw_audio_key(jax.random.fold_in(jax.random.fold_in(arg_keys[13], part), 71), part)
    audio_value = bell_draw(part_splits[5], (BATCH, AUDIO_LEN, AUDIO_D), 1.0, 6.0, ((0, 2), (1, 4), (2, 2)))
    audio_query = draw_audio_query(jax.random.fold_in(jax.random.fold_in(arg_keys[13], part), 71), part)
    cross_key = draw_cross_key(jax.random.fold_in(jax.random.fold_in(arg_keys[13], part), 71), part)
    cross_value = bell_draw(part_splits[8], (BATCH, VIDEO_LEN, AUDIO_D), 1.0, 6.0, ((0, 2), (1, 4), (2, 2)))
    audio_input = jnp.clip(jax.random.uniform(part_splits[9], (BATCH, AUDIO_LEN, AUDIO_D), jnp.float32, -0.29882812, 0.29882812) * steps_of(part_splits[9], (BATCH, AUDIO_LEN, AUDIO_D), ((0, 2), (1, 4)), -0.4, 0.0), -0.29882812, 0.29882812).astype(jnp.bfloat16)
    norm_gain = jnp.clip(1.0 + 0.18 * jax.random.normal(arg_keys[10], (AUDIO_D,), jnp.float32), 0.1, 1.9)
    up_weight = bell_draw(arg_keys[11], (AUDIO_D, FFA), AUDIO_D ** -0.5, 0.125, ((0, 2), (1, 4)))
    down_weight = bell_draw(arg_keys[12], (FFA, AUDIO_D), FFA ** -0.5, 0.0625, ((0, 4), (1, 2)))
    return dict(video_query=video_query, video_key=video_key, video_value=video_value, cross_query=cross_query, audio_key=audio_key, audio_value=audio_value, audio_query=audio_query, cross_key=cross_key, cross_value=cross_value, audio_input=audio_input, norm_gain=norm_gain, up_weight=up_weight, down_weight=down_weight)


def attend_rows(queries, keys_in, values_in, head_count):
    head_size = queries.shape[1] // head_count
    query_heads = queries.reshape(queries.shape[0], head_count, head_size).astype(jnp.float32)
    key_heads = keys_in.reshape(keys_in.shape[0], head_count, head_size).astype(jnp.float32)
    value_heads = values_in.reshape(values_in.shape[0], head_count, head_size).astype(jnp.float32)
    scores = jnp.einsum('qhd,khd->qhk', query_heads, key_heads) / math.sqrt(head_size)
    peak_value = lax.optimization_barrier(jnp.max(scores, axis=2, keepdims=True))
    weights = jnp.exp(scores - peak_value)
    totals = lax.optimization_barrier(jnp.sum(weights, axis=2))
    rounded = lax.optimization_barrier(weights.astype(jnp.bfloat16)).astype(jnp.float32)
    weighted = jnp.einsum('qhk,khd->qhd', rounded, value_heads)
    result = weighted / totals[:, :, None]
    return result.reshape(queries.shape[0], head_count * head_size).astype(jnp.bfloat16)

def attend(queries, keys_in, values_in, head_count):
    row_total = queries.shape[0]
    block_rows = 512 if row_total % 512 == 0 else row_total
    pieces = queries.reshape(row_total // block_rows, block_rows, queries.shape[1])
    result = lax.map(lambda row_piece: attend_rows(row_piece, keys_in, values_in, head_count), pieces)
    return result.reshape(row_total, queries.shape[1])

def reference(video_query, video_key, video_value, cross_query, audio_key, audio_value, audio_query, cross_key, cross_value, audio_input, norm_gain, up_weight, down_weight):
    mixed_list, heard_list, seen_list, output_list = ([], [], [], [])
    for sample in range(BATCH):
        mixed_list.append(attend(video_query[sample], video_key[sample], video_value[sample], VHEADS))
        heard_list.append(attend(cross_query[sample], audio_key[sample], audio_value[sample], CHEADS))
        audio_seen = attend(audio_query[sample], cross_key[sample], cross_value[sample], CHEADS)
        seen_list.append(audio_seen)
        residual = audio_input[sample].astype(jnp.float32) + audio_seen.astype(jnp.float32)
        scale_factor = lax.rsqrt(lax.optimization_barrier(jnp.mean(residual * residual, axis=1, keepdims=True)) + 1e-06)
        normed = (residual * scale_factor * norm_gain.astype(jnp.float32)).astype(jnp.bfloat16)
        hidden = jax.nn.gelu(jnp.dot(normed, up_weight, preferred_element_type=jnp.float32)).astype(jnp.bfloat16)
        output_list.append(jnp.dot(hidden, down_weight, preferred_element_type=jnp.float32).astype(jnp.bfloat16))
    return (jnp.stack(mixed_list), jnp.stack(heard_list), jnp.stack(seen_list), jnp.stack(output_list))
```

```python
import functools
import math

import jax
import jax.numpy as jnp
from jax import lax
from jax.experimental import pallas as pl
from jax.experimental.pallas import tpu as pltpu
from jax.sharding import PartitionSpec as P

VHEAD = 128
CHEAD = 64
MESH = pl.DeviceIdType.MESH
LOG2E = math.log2(math.e)
CHUNKS = 4


def dot_t(a, b):
    return lax.dot_general(a, b, (((1,), (1,)), ((), ())), preferred_element_type=jnp.float32)


def softmax_parts(q, k, scale):
    s = dot_t(q, k)
    peak = jnp.max(s, axis=1, keepdims=True)
    p = jnp.exp2((s - peak) * (scale * LOG2E))
    return p, peak * scale, jnp.sum(p, axis=1, keepdims=True)


def pair_attend(q, k, v, scale):
    low = lax.broadcasted_iota(jnp.int32, q.shape, 1) < CHEAD
    zero = jnp.zeros_like(q)
    both = jnp.concatenate([jnp.where(low, q, zero), jnp.where(low, zero, q)], axis=0)
    p, peak, total = softmax_parts(both, k, scale)
    o = jnp.dot(p.astype(jnp.bfloat16), v, preferred_element_type=jnp.float32)
    return o, peak, total


def fused_kernel(
    n, tp,
    vq, vk, vv, cq, ak, av, aq, ck, cv, ai, gain, up, down,
    mixed, heard, seen, mlp,
    qbuf, kbuf, vbuf, obuf, abuf, cqv, ckv, cvv, upv, downv, xsend, xrecv, ssbuf, nbuf, pbuf, rsend, rrecv,
    v_send, v_recv, o_send, o_recv, a_send, a_recv, x_send, x_recv, s_send, s_recv,
    n_send, n_recv, p_send, p_recv, r_send, r_recv, own_sem, oown_sem, load_sem,
):
    me = lax.axis_index("seq")
    col = lax.axis_index("tp")
    tokens = vq.shape[0]
    hd = vq.shape[1] // VHEAD // n
    rows, width = aq.shape
    pairs = width // 128
    units = up.shape[1]
    step = units // CHUNKS
    f32, bf16 = jnp.float32, jnp.bfloat16
    peers = [lax.rem(me + d, n) for d in range(1, n)]
    tp_peers = [lax.rem(col + d, tp) for d in range(1, tp)]

    def remote(src, dst, ss, rs, where):
        copy = pltpu.make_async_remote_copy(
            src_ref=src, dst_ref=dst, send_sem=ss, recv_sem=rs, device_id=where, device_id_type=MESH
        )
        copy.start()
        return copy

    loads = []
    for i, (src, dst) in enumerate(((ck, ckv), (cv, cvv), (cq, cqv), (up, upv), (down, downv))):
        loads.append(pltpu.make_async_copy(src, dst, load_sem.at[i]))
        loads[-1].start()
    owns = []
    for h in range(hd):
        cols = pl.ds(pl.multiple_of((me * hd + h) * VHEAD, VHEAD), VHEAD)
        owns.append([])
        for i, (src, buf) in enumerate(((vq, qbuf), (vk, kbuf), (vv, vbuf))):
            copy = pltpu.make_async_copy(src.at[:, cols], buf.at[h, me], own_sem.at[h, i])
            copy.start()
            owns[-1].append(copy)

    barrier = pltpu.get_barrier_semaphore()
    for p in peers:
        pl.semaphore_signal(barrier, inc=1, device_id={"seq": p}, device_id_type=MESH)
    for t in tp_peers:
        pl.semaphore_signal(barrier, inc=1, device_id={"tp": t}, device_id_type=MESH)
    pl.semaphore_wait(barrier, n - 1 + tp - 1)

    sent = []

    def send_video(h):
        copies = []
        for d, p in enumerate(peers):
            cols = pl.ds(pl.multiple_of((p * hd + h) * VHEAD, VHEAD), VHEAD)
            for i, (src, buf) in enumerate(((vq, qbuf), (vk, kbuf), (vv, vbuf))):
                copies.append(
                    remote(src.at[:, cols], buf.at[h, me], v_send.at[h, d, i], v_recv.at[h, d, i], {"seq": p})
                )
        sent.extend(copies)
        return copies

    def attend_video(h, copies):
        for copy in owns[h]:
            copy.wait()
        for copy in copies:
            copy.wait_recv()
        k = kbuf[h].reshape(n * tokens, VHEAD)
        v = vbuf[h].reshape(n * tokens, VHEAD)
        cols = pl.ds(pl.multiple_of((me * hd + h) * VHEAD, VHEAD), VHEAD)
        out = []
        for d in range(1, n + 1):
            p = lax.rem(me + d, n)
            w, _, total = softmax_parts(qbuf[h, p], k, 1.0 / math.sqrt(VHEAD))
            o = jnp.dot(w.astype(bf16), v, preferred_element_type=f32) / total
            obuf[h, p] = o.astype(bf16)
            if d < n:
                out.append(
                    remote(obuf.at[h, p], mixed.at[:, cols], o_send.at[h, d - 1], o_recv.at[h, d - 1], {"seq": p})
                )
        own = pltpu.make_async_copy(obuf.at[h, me], mixed.at[:, cols], oown_sem.at[h])
        own.start()
        return out, own

    gathers = []
    for i, src in enumerate((aq, ak, av)):
        for d, p in enumerate(peers):
            gathers.append(remote(src, abuf.at[i, me], a_send.at[i, d], a_recv.at[i, d], {"seq": p}))
        abuf[i, me] = src[...]
    sent.extend(gathers)
    video = [send_video(0)]

    for copy in loads[:2]:
        copy.wait()
    for copy in gathers:
        copy.wait_recv()

    def whole(i):
        return jnp.concatenate([abuf[i, s].astype(f32) for s in range(n)], axis=0).astype(bf16)

    scale = 1.0 / math.sqrt(CHEAD)
    total_rows = n * rows
    q_all = whole(0)
    lane = lax.broadcasted_iota(jnp.int32, (total_rows, 128), 1)
    peaks = jnp.zeros((total_rows, 128), f32)
    totals = jnp.ones((total_rows, 128), f32)
    for j in range(pairs):
        at = slice(j * 128, (j + 1) * 128)
        o, peak, total = pair_attend(q_all[:, at], ckv[:, at], cvv[:, at], scale)
        picked = jnp.where(lane < CHEAD, o[:total_rows], o[total_rows:])
        xsend[:, :, at] = picked.reshape(n, rows, 128)
        for half in range(2):
            part = slice(half * total_rows, (half + 1) * total_rows)
            peaks = jnp.where(lane == 2 * j + half, peak[part], peaks)
            totals = jnp.where(lane == 2 * j + half, total[part], totals)
    xsend[:, :, width : width + 128] = peaks.reshape(n, rows, 128)
    xsend[:, :, width + 128 : width + 256] = totals.reshape(n, rows, 128)
    exchanges = []
    for d, p in enumerate(peers):
        exchanges.append(remote(xsend.at[p], xrecv.at[me], x_send.at[d], x_recv.at[d], {"seq": p}))
    sent.extend(exchanges)
    xrecv[me] = xsend[me]
    for h in range(1, min(2, hd)):
        video.append(send_video(h))

    loads[2].wait()
    k_all, v_all = whole(1), whole(2)
    wide = lax.broadcasted_iota(jnp.int32, (tokens, 128), 1)
    for j in range(pairs):
        at = slice(j * 128, (j + 1) * 128)
        o, _, total = pair_attend(cqv[:, at], k_all[:, at], v_all[:, at], scale)
        o = o / total
        heard[:, at] = jnp.where(wide < CHEAD, o[:tokens], o[tokens:]).astype(bf16)

    for copy in exchanges:
        copy.wait_recv()
    peak = xrecv[0, :, width : width + 128]
    for s in range(1, n):
        peak = jnp.maximum(peak, xrecv[s, :, width : width + 128])
    factors = [jnp.exp(xrecv[s, :, width : width + 128] - peak) for s in range(n)]
    total = sum(factors[s] * xrecv[s, :, width + 128 : width + 256] for s in range(n))
    factors = [f / total for f in factors]
    low = lax.broadcasted_iota(jnp.int32, (rows, 128), 1) < CHEAD
    pieces = []
    for j in range(pairs):
        at = slice(j * 128, (j + 1) * 128)
        value = jnp.zeros((rows, 128), f32)
        for s in range(n):
            f = factors[s]
            value += jnp.where(low, f[:, 2 * j : 2 * j + 1], f[:, 2 * j + 1 : 2 * j + 2]) * xrecv[s, :, at]
        pieces.append(value)
    seen_bf = jnp.concatenate(pieces, axis=1).astype(bf16)
    seen[...] = seen_bf

    mine = pl.ds(pl.multiple_of(col * width, 128), width)
    residual = ai[:, mine].astype(f32) + seen_bf.astype(f32)
    square = jnp.sum(residual * residual, axis=1, keepdims=True)
    ssbuf[col] = jnp.broadcast_to(square, (rows, 128))
    squares = []
    for d, t in enumerate(tp_peers):
        squares.append(remote(ssbuf.at[col], ssbuf.at[col], s_send.at[d], s_recv.at[d], {"tp": t}))
    sent.extend(squares)
    for copy in squares:
        copy.wait_recv()
    square = sum(ssbuf[t] for t in range(tp))[:, 0:1]
    factor = lax.rsqrt(square / (width * tp) + 1e-6)
    nbuf[me] = (residual * factor * gain[:, mine]).astype(bf16)
    normed = []
    for d, p in enumerate(peers):
        normed.append(remote(nbuf.at[me], nbuf.at[me], n_send.at[d], n_recv.at[d], {"seq": p}))
    sent.extend(normed)
    for h in range(2, min(3, hd)):
        video.append(send_video(h))

    outs = [attend_video(0, video[0])]

    loads[3].wait()
    for copy in normed:
        copy.wait_recv()
    x = jnp.concatenate([nbuf[s].astype(f32) for s in range(n)], axis=0).astype(bf16)
    partials = []
    for c in range(CHUNKS):
        pbuf[col, c] = jnp.dot(x, upv[:, c * step : (c + 1) * step], preferred_element_type=f32)
        for d, t in enumerate(tp_peers):
            partials.append(
                remote(pbuf.at[col, c], pbuf.at[col, c], p_send.at[c, d], p_recv.at[c, d], {"tp": t})
            )
    sent.extend(partials)
    for h in range(3, hd):
        video.append(send_video(h))

    if hd > 1:
        outs.append(attend_video(1, video[1]))

    loads[4].wait()
    for copy in partials:
        copy.wait_recv()
    acc = jnp.zeros((total_rows, width), f32)
    for c in range(CHUNKS):
        hidden = jax.nn.gelu(sum(pbuf[t, c] for t in range(tp)), approximate=True).astype(bf16)
        acc += jnp.dot(hidden, downv[c * step : (c + 1) * step, :], preferred_element_type=f32)
    rsend[...] = acc.reshape(n, rows, width)
    results = []
    for d, p in enumerate(peers):
        results.append(remote(rsend.at[p], rrecv.at[me], r_send.at[d], r_recv.at[d], {"seq": p}))
    sent.extend(results)
    rrecv[me] = rsend[me]

    for h in range(2, hd):
        outs.append(attend_video(h, video[h]))

    for copy in results:
        copy.wait_recv()
    mlp[...] = sum(rrecv[s] for s in range(n)).astype(bf16)

    for out, own in outs:
        for copy in out:
            copy.wait()
        own.wait()
    for copy in sent:
        copy.wait_send()


def fused(n, tp, args):
    vq, vk, vv, cq, ak, av, aq, ck, cv, ai, gain, up, down = args
    tokens, vwidth = vq.shape
    hd = vwidth // VHEAD // n
    rows, width = aq.shape
    units = up.shape[1]
    bf16, f32 = jnp.bfloat16, jnp.float32
    anywhere = pl.BlockSpec(memory_space=pl.ANY)
    vmem = pl.BlockSpec(memory_space=pltpu.VMEM)
    dma = pltpu.SemaphoreType.DMA
    head = pltpu.VMEM((hd, n, tokens, VHEAD), bf16)
    cross = pltpu.VMEM((tokens, width), bf16)
    z, t = max(n - 1, 1), max(tp - 1, 1)
    return pl.pallas_call(
        functools.partial(fused_kernel, n, tp),
        out_shape=(
            jax.ShapeDtypeStruct((tokens, vwidth), bf16),
            jax.ShapeDtypeStruct((tokens, width), bf16),
            jax.ShapeDtypeStruct((rows, width), bf16),
            jax.ShapeDtypeStruct((rows, width), bf16),
        ),
        in_specs=[anywhere] * 4 + [vmem] * 3 + [anywhere] * 2 + [vmem] * 2 + [anywhere] * 2,
        out_specs=(anywhere, vmem, vmem, vmem),
        scratch_shapes=[
            head, head, head, head,
            pltpu.VMEM((3, n, rows, width), bf16),
            cross, cross, cross,
            pltpu.VMEM(up.shape, bf16),
            pltpu.VMEM(down.shape, bf16),
            pltpu.VMEM((n, rows, width + 256), f32),
            pltpu.VMEM((n, rows, width + 256), f32),
            pltpu.VMEM((tp, rows, 128), f32),
            pltpu.VMEM((n, rows, width), bf16),
            pltpu.VMEM((tp, CHUNKS, n * rows, units // CHUNKS), f32),
            pltpu.VMEM((n, rows, width), f32),
            pltpu.VMEM((n, rows, width), f32),
            dma((hd, z, 3)), dma((hd, z, 3)), dma((hd, z)), dma((hd, z)),
            dma((3, z)), dma((3, z)), dma((z,)), dma((z,)), dma((t,)), dma((t,)),
            dma((z,)), dma((z,)), dma((CHUNKS, t)), dma((CHUNKS, t)), dma((z,)), dma((z,)),
            dma((hd, 3)), dma((hd,)), dma((5,)),
        ],
        compiler_params=pltpu.CompilerParams(collective_id=0, has_side_effects=True),
    )(vq, vk, vv, cq, ak, av, aq, ck, cv, ai, gain.reshape(1, -1), up, down)


def fits(n, vq, aq, up):
    heads = vq.shape[2] // VHEAD
    return (
        heads % n == 0
        and vq.shape[1] % 16 == 0
        and aq.shape[1] % 8 == 0
        and aq.shape[2] % 128 == 0
        and aq.shape[2] // CHEAD <= 128
        and up.shape[0] == aq.shape[2]
        and up.shape[1] % (128 * CHUNKS) == 0
    )


def attend_rows(queries, keys_in, values_in, head_count):
    head_size = queries.shape[1] // head_count
    query_heads = queries.reshape(queries.shape[0], head_count, head_size)
    key_heads = keys_in.reshape(keys_in.shape[0], head_count, head_size)
    value_heads = values_in.reshape(values_in.shape[0], head_count, head_size)
    scores = jnp.einsum(
        "qhd,khd->qhk", query_heads, key_heads, preferred_element_type=jnp.float32
    ) / math.sqrt(head_size)
    peak_value = jnp.max(scores, axis=2, keepdims=True)
    weights = jnp.exp(scores - peak_value)
    totals = jnp.sum(weights, axis=2)
    weighted = jnp.einsum(
        "qhk,khd->qhd",
        weights.astype(jnp.bfloat16),
        value_heads,
        preferred_element_type=jnp.float32,
    )
    result = weighted / totals[:, :, None]
    return result.reshape(queries.shape[0], head_count * head_size).astype(jnp.bfloat16)


def attend(queries, keys_in, values_in, head_count):
    row_total = queries.shape[0]
    block_rows = 512 if row_total % 512 == 0 else row_total
    pieces = queries.reshape(row_total // block_rows, block_rows, queries.shape[1])
    result = lax.map(
        lambda row_piece: attend_rows(row_piece, keys_in, values_in, head_count), pieces
    )
    return result.reshape(row_total, queries.shape[1])


def video_self(queries, keys_in, values_in):
    seq_count = lax.axis_size("seq")
    local_heads = queries.shape[1] // VHEAD
    dest_heads = max(local_heads // seq_count, 1)
    blocks = seq_count * dest_heads // local_heads
    groups = local_heads // dest_heads
    group_width = dest_heads * VHEAD
    token_count = queries.shape[0]
    block_tokens = token_count // blocks

    def spread(tensor):
        shaped = tensor.reshape(token_count, groups, group_width).transpose(1, 0, 2)
        shaped = jnp.broadcast_to(shaped[:, None], (groups, blocks, token_count, group_width))
        return shaped.reshape(seq_count, token_count, group_width)

    shaped = queries.reshape(blocks, block_tokens, groups, group_width).transpose(2, 0, 1, 3)
    own_queries = lax.all_to_all(
        shaped.reshape(seq_count, block_tokens, group_width),
        "seq",
        split_axis=0,
        concat_axis=0,
        tiled=True,
    )
    keys_all = lax.all_to_all(spread(keys_in), "seq", split_axis=0, concat_axis=0, tiled=True)
    values_all = lax.all_to_all(spread(values_in), "seq", split_axis=0, concat_axis=0, tiled=True)
    keys_all = keys_all.reshape(-1, group_width)
    values_all = values_all.reshape(-1, group_width)
    own_queries = own_queries.reshape(-1, group_width)
    attended = attend(own_queries, keys_all, values_all, dest_heads)
    returned = lax.all_to_all(
        attended.reshape(seq_count, block_tokens, group_width),
        "seq",
        split_axis=0,
        concat_axis=0,
        tiled=True,
    )
    returned = returned.reshape(groups, blocks, block_tokens, group_width).transpose(1, 2, 0, 3)
    return returned.reshape(token_count, groups * group_width)


def audio_listen(queries, keys_in, values_in, head_count):
    head_size = queries.shape[1] // head_count
    query_heads = queries.reshape(queries.shape[0], head_count, head_size)
    key_heads = keys_in.reshape(keys_in.shape[0], head_count, head_size)
    value_heads = values_in.reshape(values_in.shape[0], head_count, head_size)
    scores = jnp.einsum(
        "qhd,khd->qhk", query_heads, key_heads, preferred_element_type=jnp.float32
    ) / math.sqrt(head_size)
    local_peak = jnp.max(scores, axis=2)
    peak_value = lax.pmax(local_peak, "seq")
    weights = jnp.exp(scores - peak_value[:, :, None])
    totals = jnp.sum(weights, axis=2)
    weighted = jnp.einsum(
        "qhk,khd->qhd",
        weights.astype(jnp.bfloat16),
        value_heads,
        preferred_element_type=jnp.float32,
    )
    totals, weighted = (totals, weighted.reshape(queries.shape[0], head_count * head_size))
    totals, weighted = (
        lax.psum_scatter(totals, "seq", scatter_dimension=0, tiled=True),
        lax.psum_scatter(weighted, "seq", scatter_dimension=0, tiled=True),
    )
    return (weighted / jnp.repeat(totals, head_size, axis=1)).astype(jnp.bfloat16)


def audio_block(audio_rows, audio_seen, norm_gain, up_weight, down_weight):
    features = lax.all_gather(audio_seen, "tp", axis=1, tiled=True)
    residual = audio_rows.astype(jnp.float32) + features.astype(jnp.float32)
    scale_factor = lax.rsqrt(jnp.mean(residual * residual, axis=1, keepdims=True) + 1e-06)
    normed = (residual * scale_factor * norm_gain).astype(jnp.bfloat16)
    slice_width = up_weight.shape[0]
    own_features = lax.dynamic_slice_in_dim(
        normed, lax.axis_index("tp") * slice_width, slice_width, 1
    )
    partial_sum = jnp.dot(
        lax.all_gather(own_features, "seq", axis=0, tiled=True),
        up_weight,
        preferred_element_type=jnp.float32,
    )
    hidden = jax.nn.gelu(lax.psum(partial_sum, "tp")).astype(jnp.bfloat16)
    return lax.psum_scatter(
        jnp.dot(hidden, down_weight, preferred_element_type=jnp.float32),
        "seq",
        scatter_dimension=0,
        tiled=True,
    ).astype(jnp.bfloat16)


def body(
    video_query,
    video_key,
    video_value,
    cross_query,
    audio_key,
    audio_value,
    audio_query,
    cross_key,
    cross_value,
    audio_input,
    norm_gain,
    up_weight,
    down_weight,
):
    if fits(lax.axis_size("seq"), video_query, audio_query, up_weight):
        args = (video_query, video_key, video_value, cross_query, audio_key, audio_value)
        args += (audio_query, cross_key, cross_value, audio_input)
        args = tuple(a[0] for a in args) + (norm_gain, up_weight, down_weight)
        outs = fused(lax.axis_size("seq"), lax.axis_size("tp"), args)
        return tuple(out[None] for out in outs)
    mixed_list, heard_list, seen_list, output_list = ([], [], [], [])
    cross_heads = cross_query.shape[2] // CHEAD
    mixed_list.append(video_self(video_query[0], video_key[0], video_value[0]))
    gathered_query = lax.all_gather(audio_query[0], "seq", axis=0, tiled=True)
    gathered_key = lax.all_gather(audio_key[0], "seq", axis=0, tiled=True)
    gathered_value = lax.all_gather(audio_value[0], "seq", axis=0, tiled=True)
    heard_list.append(attend(cross_query[0], gathered_key, gathered_value, cross_heads))
    audio_seen = audio_listen(gathered_query, cross_key[0], cross_value[0], cross_heads)
    seen_list.append(audio_seen)
    output_list.append(audio_block(audio_input[0], audio_seen, norm_gain, up_weight, down_weight))
    return (
        jnp.stack(mixed_list),
        jnp.stack(heard_list),
        jnp.stack(seen_list),
        jnp.stack(output_list),
    )


def solution(mesh):
    placed = (
        P(("clips", "dp"), "seq", "tp"),
        P(("clips", "dp"), "seq", "tp"),
        P(("clips", "dp"), "seq", "tp"),
        P(("clips", "dp"), "seq", "tp"),
        P(("clips", "dp"), "seq", "tp"),
        P(("clips", "dp"), "seq", "tp"),
        P(("clips", "dp"), "seq", "tp"),
        P(("clips", "dp"), "seq", "tp"),
        P(("clips", "dp"), "seq", "tp"),
        P(("clips", "dp"), "seq", None),
        P(),
        P("tp", "seq"),
        P("seq", "tp"),
    )
    return jax.shard_map(
        body,
        mesh=mesh,
        in_specs=placed,
        out_specs=(
            P(("clips", "dp"), "seq", "tp"),
            P(("clips", "dp"), "seq", "tp"),
            P(("clips", "dp"), "seq", "tp"),
            P(("clips", "dp"), "seq", "tp"),
        ),
        check_vma=False,
    )
```

```python
import functools
import math

import jax
import jax.numpy as jnp
from jax import lax
from jax.experimental import pallas as pl
from jax.experimental.pallas import tpu as pltpu
from jax.sharding import PartitionSpec as P

VHEAD = 128
CHEAD = 64
MESH = pl.DeviceIdType.MESH
LOG2E = math.log2(math.e)
CHUNKS = 4


def dot_t(a, b):
    return lax.dot_general(a, b, (((1,), (1,)), ((), ())), preferred_element_type=jnp.float32)


def softmax_parts(q, k, scale):
    s = dot_t(q, k)
    peak = jnp.max(s, axis=1, keepdims=True)
    p = jnp.exp2((s - peak) * (scale * LOG2E))
    return p, peak * scale, jnp.sum(p, axis=1, keepdims=True)


def pair_attend(q, k, v, scale):
    low = lax.broadcasted_iota(jnp.int32, q.shape, 1) < CHEAD
    zero = jnp.zeros_like(q)
    both = jnp.concatenate([jnp.where(low, q, zero), jnp.where(low, zero, q)], axis=0)
    p, peak, total = softmax_parts(both, k, scale)
    o = jnp.dot(p.astype(jnp.bfloat16), v, preferred_element_type=jnp.float32)
    return o, peak, total


def partners(me, n):
    if n & (n - 1):
        return [lax.rem(me + d, n) for d in range(1, n)]
    found = []
    for flip in range(n - 1, 0, -1):
        place, bit = me * 0, 1
        while bit < n:
            digit = lax.rem(lax.div(me, bit), 2)
            place = place + bit * ((1 - digit) if flip & bit else digit)
            bit *= 2
        found.append(place)
    return found


def fused_kernel(
    n, tp,
    vq, vk, vv, cq, ak, av, aq, ck, cv, ai, gain, up, down,
    mixed, heard, seen, mlp,
    qbuf, kbuf, vbuf, obuf, abuf, cqv, ckv, cvv, upv, downv, xsend, xrecv, tsend, trecv, hbuf, sbuf, mbuf, ssbuf, nbuf, pbuf, rsend, rrecv,
    v_send, v_recv, o_send, o_recv, a_send, a_recv, x_send, x_recv, t_send, t_recv, s_send, s_recv,
    n_send, n_recv, p_send, p_recv, r_send, r_recv, own_sem, oown_sem, load_sem,
):
    me = lax.axis_index("seq")
    col = lax.axis_index("tp")
    tokens = vq.shape[0]
    hd = vq.shape[1] // VHEAD // n
    rows, width = aq.shape
    pairs = width // 128
    units = up.shape[1]
    step = units // CHUNKS
    f32, bf16 = jnp.float32, jnp.bfloat16
    peers = partners(me, n)
    tp_peers = [lax.rem(col + d, tp) for d in range(1, tp)]

    def remote(src, dst, ss, rs, where):
        copy = pltpu.make_async_remote_copy(
            src_ref=src, dst_ref=dst, send_sem=ss, recv_sem=rs, device_id=where, device_id_type=MESH
        )
        copy.start()
        return copy

    loads = []
    for i, (src, dst) in enumerate(((ck, ckv), (cv, cvv), (cq, cqv), (up, upv), (down, downv))):
        loads.append(pltpu.make_async_copy(src, dst, load_sem.at[i]))
        loads[-1].start()
    owns = []
    for h in range(hd):
        cols = pl.ds(pl.multiple_of((me * hd + h) * VHEAD, VHEAD), VHEAD)
        owns.append([])
        for i, (src, buf) in enumerate(((vq, qbuf), (vk, kbuf), (vv, vbuf))):
            copy = pltpu.make_async_copy(src.at[:, cols], buf.at[h, me], own_sem.at[h, i])
            copy.start()
            owns[-1].append(copy)

    barrier = pltpu.get_barrier_semaphore()
    for p in peers:
        pl.semaphore_signal(barrier, inc=1, device_id={"seq": p}, device_id_type=MESH)
    for t in tp_peers:
        pl.semaphore_signal(barrier, inc=1, device_id={"tp": t}, device_id_type=MESH)
    pl.semaphore_wait(barrier, n - 1 + tp - 1)

    sent = []

    def send_video(h):
        copies = []
        for d, p in enumerate(peers):
            cols = pl.ds(pl.multiple_of((p * hd + h) * VHEAD, VHEAD), VHEAD)
            for i, (src, buf) in enumerate(((vq, qbuf), (vk, kbuf), (vv, vbuf))):
                copies.append(
                    remote(src.at[:, cols], buf.at[h, me], v_send.at[h, d, i], v_recv.at[h, d, i], {"seq": p})
                )
        sent.extend(copies)
        return copies

    def attend_video(h, copies):
        for copy in owns[h]:
            copy.wait()
        for copy in copies:
            copy.wait_recv()
        k = kbuf[h].reshape(n * tokens, VHEAD)
        v = vbuf[h].reshape(n * tokens, VHEAD)
        cols = pl.ds(pl.multiple_of((me * hd + h) * VHEAD, VHEAD), VHEAD)
        out = []
        for d, p in enumerate(peers + [me]):
            w, _, total = softmax_parts(qbuf[h, p], k, 1.0 / math.sqrt(VHEAD))
            o = jnp.dot(w.astype(bf16), v, preferred_element_type=f32) / total
            obuf[h, p] = o.astype(bf16)
            if d < n - 1:
                out.append(remote(obuf.at[h, p], mixed.at[:, cols], o_send.at[h, d], o_recv.at[h, d], {"seq": p}))
        own = pltpu.make_async_copy(obuf.at[h, me], mixed.at[:, cols], oown_sem.at[h])
        own.start()
        return out, own

    relay = n == 4
    gathers, direct = [], []
    for i, src in enumerate((aq, ak, av)):
        for d, p in enumerate(peers):
            if i == 0 or not relay or d > 0:
                copy = remote(src, abuf.at[i, me], a_send.at[i, d], a_recv.at[i, d], {"seq": p})
                (direct if i else gathers).append(copy)
        abuf[i, me] = src[...]
    sent.extend(gathers + direct)
    video = [send_video(0)]

    for copy in loads[:2]:
        copy.wait()
    for copy in gathers:
        copy.wait_recv()

    def whole(i):
        return jnp.concatenate([abuf[i, s].astype(f32) for s in range(n)], axis=0).astype(bf16)

    scale = 1.0 / math.sqrt(CHEAD)
    total_rows = n * rows
    q_all = whole(0)
    lane = lax.broadcasted_iota(jnp.int32, (total_rows, 128), 1)
    stats = jnp.ones((total_rows, 128), f32)
    for j in range(pairs):
        at = slice(j * 128, (j + 1) * 128)
        o, peak, total = pair_attend(q_all[:, at], ckv[:, at], cvv[:, at], scale)
        picked = jnp.where(lane < CHEAD, o[:total_rows], o[total_rows:])
        xsend[:, :, at] = picked.reshape(n, rows, 128).astype(bf16)
        for half in range(2):
            part = slice(half * total_rows, (half + 1) * total_rows)
            stats = jnp.where(lane == 2 * j + half, peak[part], stats)
            stats = jnp.where(lane == 64 + 2 * j + half, total[part], stats)
    tsend[...] = stats.reshape(n, rows, 128)
    exchanges = []
    for d, p in enumerate(peers):
        exchanges.append(remote(tsend.at[p], trecv.at[me], t_send.at[d], t_recv.at[d], {"seq": p}))
        exchanges.append(remote(xsend.at[p], xrecv.at[me], x_send.at[d], x_recv.at[d], {"seq": p}))
    sent.extend(exchanges)
    xrecv[me] = xsend[me]
    trecv[me] = tsend[me]
    for h in range(1, min(2, hd)):
        video.append(send_video(h))

    loads[2].wait()
    for copy in direct:
        copy.wait_recv()
    if relay:
        passed = []
        for i in (1, 2):
            slot = abuf.at[i, peers[1]]
            passed.append(remote(slot, slot, a_send.at[i, 0], a_recv.at[i, 0], {"seq": peers[2]}))
        sent.extend(passed)
        for copy in passed:
            copy.wait_recv()
    k_all, v_all = whole(1), whole(2)
    wide = lax.broadcasted_iota(jnp.int32, (tokens, 128), 1)
    for j in range(pairs):
        at = slice(j * 128, (j + 1) * 128)
        o, _, total = pair_attend(cqv[:, at], k_all[:, at], v_all[:, at], scale)
        o = o / total
        hbuf[:, at] = jnp.where(wide < CHEAD, o[:tokens], o[tokens:]).astype(bf16)
    results_out = [pltpu.make_async_copy(hbuf, heard, load_sem.at[5])]
    results_out[-1].start()

    for copy in exchanges:
        copy.wait_recv()
    peak = trecv[0]
    for s in range(1, n):
        peak = jnp.maximum(peak, trecv[s])
    factors = [jnp.exp(trecv[s] - peak) for s in range(n)]
    total = sum(factors[s] * pltpu.roll(trecv[s], 64, 1) for s in range(n))
    factors = [f / total for f in factors]
    low = lax.broadcasted_iota(jnp.int32, (rows, 128), 1) < CHEAD
    pieces = []
    for j in range(pairs):
        at = slice(j * 128, (j + 1) * 128)
        value = jnp.zeros((rows, 128), f32)
        for s in range(n):
            f = factors[s]
            value += jnp.where(low, f[:, 2 * j : 2 * j + 1], f[:, 2 * j + 1 : 2 * j + 2]) * xrecv[s, :, at].astype(f32)
        pieces.append(value)
    seen_bf = jnp.concatenate(pieces, axis=1).astype(bf16)
    sbuf[...] = seen_bf
    results_out.append(pltpu.make_async_copy(sbuf, seen, load_sem.at[6]))
    results_out[-1].start()

    mine = pl.ds(pl.multiple_of(col * width, 128), width)
    residual = ai[:, mine].astype(f32) + seen_bf.astype(f32)
    square = jnp.sum(residual * residual, axis=1, keepdims=True)
    ssbuf[col] = jnp.broadcast_to(square, (rows, 128))
    squares = []
    for d, t in enumerate(tp_peers):
        squares.append(remote(ssbuf.at[col], ssbuf.at[col], s_send.at[d], s_recv.at[d], {"tp": t}))
    sent.extend(squares)
    for copy in squares:
        copy.wait_recv()
    square = sum(ssbuf[t] for t in range(tp))[:, 0:1]
    factor = lax.rsqrt(square / (width * tp) + 1e-6)
    nbuf[me] = (residual * factor * gain[:, mine]).astype(bf16)
    normed = []
    for d, p in enumerate(peers):
        normed.append(remote(nbuf.at[me], nbuf.at[me], n_send.at[d], n_recv.at[d], {"seq": p}))
    sent.extend(normed)
    for h in range(2, min(3, hd)):
        video.append(send_video(h))

    outs = [attend_video(0, video[0])]

    loads[3].wait()
    for copy in normed:
        copy.wait_recv()
    x = jnp.concatenate([nbuf[s].astype(f32) for s in range(n)], axis=0).astype(bf16)
    partials = []
    for c in range(CHUNKS):
        pbuf[col, c] = jnp.dot(x, upv[:, c * step : (c + 1) * step], preferred_element_type=f32)
        for d, t in enumerate(tp_peers):
            partials.append(
                remote(pbuf.at[col, c], pbuf.at[col, c], p_send.at[c, d], p_recv.at[c, d], {"tp": t})
            )
    sent.extend(partials)
    for h in range(3, hd):
        video.append(send_video(h))

    if hd > 1:
        outs.append(attend_video(1, video[1]))

    loads[4].wait()
    for copy in partials:
        copy.wait_recv()
    acc = jnp.zeros((total_rows, width), f32)
    for c in range(CHUNKS):
        hidden = jax.nn.gelu(sum(pbuf[t, c] for t in range(tp)), approximate=True).astype(bf16)
        acc += jnp.dot(hidden, downv[c * step : (c + 1) * step, :], preferred_element_type=f32)
    rsend[...] = acc.reshape(n, rows, width).astype(bf16)
    results = []
    for d, p in enumerate(peers):
        results.append(remote(rsend.at[p], rrecv.at[me], r_send.at[d], r_recv.at[d], {"seq": p}))
    sent.extend(results)
    rrecv[me] = rsend[me]

    for h in range(2, hd):
        outs.append(attend_video(h, video[h]))

    for copy in results:
        copy.wait_recv()
    mbuf[...] = sum(rrecv[s].astype(f32) for s in range(n)).astype(bf16)
    results_out.append(pltpu.make_async_copy(mbuf, mlp, load_sem.at[7]))
    results_out[-1].start()

    for out, own in outs:
        for copy in out:
            copy.wait()
        own.wait()
    for copy in results_out:
        copy.wait()
    for copy in sent:
        copy.wait_send()


def fused(n, tp, args):
    vq, vk, vv, cq, ak, av, aq, ck, cv, ai, gain, up, down = args
    tokens, vwidth = vq.shape
    hd = vwidth // VHEAD // n
    rows, width = aq.shape
    units = up.shape[1]
    bf16, f32 = jnp.bfloat16, jnp.float32
    anywhere = pl.BlockSpec(memory_space=pl.ANY)
    vmem = pl.BlockSpec(memory_space=pltpu.VMEM)
    dma = pltpu.SemaphoreType.DMA
    head = pltpu.VMEM((hd, n, tokens, VHEAD), bf16)
    cross = pltpu.VMEM((tokens, width), bf16)
    z, t = max(n - 1, 1), max(tp - 1, 1)
    return pl.pallas_call(
        functools.partial(fused_kernel, n, tp),
        out_shape=(
            jax.ShapeDtypeStruct((tokens, vwidth), bf16),
            jax.ShapeDtypeStruct((tokens, width), bf16),
            jax.ShapeDtypeStruct((rows, width), bf16),
            jax.ShapeDtypeStruct((rows, width), bf16),
        ),
        in_specs=[anywhere] * 4 + [vmem] * 3 + [anywhere] * 2 + [vmem] * 2 + [anywhere] * 2,
        out_specs=(anywhere,) * 4,
        scratch_shapes=[
            head, head, head, head,
            pltpu.VMEM((3, n, rows, width), bf16),
            cross, cross, cross,
            pltpu.VMEM(up.shape, bf16),
            pltpu.VMEM(down.shape, bf16),
            pltpu.VMEM((n, rows, width), bf16),
            pltpu.VMEM((n, rows, width), bf16),
            pltpu.VMEM((n, rows, 128), f32),
            pltpu.VMEM((n, rows, 128), f32),
            cross,
            pltpu.VMEM((rows, width), bf16),
            pltpu.VMEM((rows, width), bf16),
            pltpu.VMEM((tp, rows, 128), f32),
            pltpu.VMEM((n, rows, width), bf16),
            pltpu.VMEM((tp, CHUNKS, n * rows, units // CHUNKS), f32),
            pltpu.VMEM((n, rows, width), bf16),
            pltpu.VMEM((n, rows, width), bf16),
            dma((hd, z, 3)), dma((hd, z, 3)), dma((hd, z)), dma((hd, z)),
            dma((3, z)), dma((3, z)), dma((z,)), dma((z,)), dma((z,)), dma((z,)), dma((t,)), dma((t,)),
            dma((z,)), dma((z,)), dma((CHUNKS, t)), dma((CHUNKS, t)), dma((z,)), dma((z,)),
            dma((hd, 3)), dma((hd,)), dma((8,)),
        ],
        compiler_params=pltpu.CompilerParams(collective_id=0, has_side_effects=True),
    )(vq, vk, vv, cq, ak, av, aq, ck, cv, ai, gain.reshape(1, -1), up, down)


def hand_over(*refs):
    count = (len(refs) - 2) // 3
    sources, targets, buffers = refs[:count], refs[count : 2 * count], refs[2 * count : 3 * count]
    into, out = refs[3 * count :]
    coming = [pltpu.make_async_copy(s, b, into.at[i]) for i, (s, b) in enumerate(zip(sources, buffers))]
    going = [pltpu.make_async_copy(b, t, out.at[i]) for i, (b, t) in enumerate(zip(buffers, targets))]
    for copy in coming:
        copy.start()
    for first, second in zip(coming, going):
        first.wait()
        second.start()
    for copy in going:
        copy.wait()


def deliver(arrays):
    anywhere = pl.BlockSpec(memory_space=pl.ANY)
    return pl.pallas_call(
        hand_over,
        out_shape=tuple(jax.ShapeDtypeStruct(a.shape, a.dtype) for a in arrays),
        in_specs=[anywhere] * len(arrays),
        out_specs=(anywhere,) * len(arrays),
        scratch_shapes=[pltpu.VMEM(a.shape, a.dtype) for a in arrays]
        + [pltpu.SemaphoreType.DMA((len(arrays),))] * 2,
    )(*arrays)


def fits(n, vq, aq, up):
    heads = vq.shape[2] // VHEAD
    return (
        heads % n == 0
        and vq.shape[1] % 16 == 0
        and aq.shape[1] % 8 == 0
        and aq.shape[2] % 128 == 0
        and aq.shape[2] // CHEAD <= 64
        and up.shape[0] == aq.shape[2]
        and up.shape[1] % (128 * CHUNKS) == 0
    )


def attend_rows(queries, keys_in, values_in, head_count):
    head_size = queries.shape[1] // head_count
    query_heads = queries.reshape(queries.shape[0], head_count, head_size)
    key_heads = keys_in.reshape(keys_in.shape[0], head_count, head_size)
    value_heads = values_in.reshape(values_in.shape[0], head_count, head_size)
    scores = jnp.einsum(
        "qhd,khd->qhk", query_heads, key_heads, preferred_element_type=jnp.float32
    ) / math.sqrt(head_size)
    peak_value = jnp.max(scores, axis=2, keepdims=True)
    weights = jnp.exp(scores - peak_value)
    totals = jnp.sum(weights, axis=2)
    weighted = jnp.einsum(
        "qhk,khd->qhd",
        weights.astype(jnp.bfloat16),
        value_heads,
        preferred_element_type=jnp.float32,
    )
    result = weighted / totals[:, :, None]
    return result.reshape(queries.shape[0], head_count * head_size).astype(jnp.bfloat16)


def attend(queries, keys_in, values_in, head_count):
    row_total = queries.shape[0]
    block_rows = 512 if row_total % 512 == 0 else row_total
    pieces = queries.reshape(row_total // block_rows, block_rows, queries.shape[1])
    result = lax.map(
        lambda row_piece: attend_rows(row_piece, keys_in, values_in, head_count), pieces
    )
    return result.reshape(row_total, queries.shape[1])


def video_self(queries, keys_in, values_in):
    seq_count = lax.axis_size("seq")
    local_heads = queries.shape[1] // VHEAD
    dest_heads = max(local_heads // seq_count, 1)
    blocks = seq_count * dest_heads // local_heads
    groups = local_heads // dest_heads
    group_width = dest_heads * VHEAD
    token_count = queries.shape[0]
    block_tokens = token_count // blocks

    def spread(tensor):
        shaped = tensor.reshape(token_count, groups, group_width).transpose(1, 0, 2)
        shaped = jnp.broadcast_to(shaped[:, None], (groups, blocks, token_count, group_width))
        return shaped.reshape(seq_count, token_count, group_width)

    shaped = queries.reshape(blocks, block_tokens, groups, group_width).transpose(2, 0, 1, 3)
    own_queries = lax.all_to_all(
        shaped.reshape(seq_count, block_tokens, group_width),
        "seq",
        split_axis=0,
        concat_axis=0,
        tiled=True,
    )
    keys_all = lax.all_to_all(spread(keys_in), "seq", split_axis=0, concat_axis=0, tiled=True)
    values_all = lax.all_to_all(spread(values_in), "seq", split_axis=0, concat_axis=0, tiled=True)
    keys_all = keys_all.reshape(-1, group_width)
    values_all = values_all.reshape(-1, group_width)
    own_queries = own_queries.reshape(-1, group_width)
    attended = attend(own_queries, keys_all, values_all, dest_heads)
    returned = lax.all_to_all(
        attended.reshape(seq_count, block_tokens, group_width),
        "seq",
        split_axis=0,
        concat_axis=0,
        tiled=True,
    )
    returned = returned.reshape(groups, blocks, block_tokens, group_width).transpose(1, 2, 0, 3)
    return returned.reshape(token_count, groups * group_width)


def audio_listen(queries, keys_in, values_in, head_count):
    head_size = queries.shape[1] // head_count
    query_heads = queries.reshape(queries.shape[0], head_count, head_size)
    key_heads = keys_in.reshape(keys_in.shape[0], head_count, head_size)
    value_heads = values_in.reshape(values_in.shape[0], head_count, head_size)
    scores = jnp.einsum(
        "qhd,khd->qhk", query_heads, key_heads, preferred_element_type=jnp.float32
    ) / math.sqrt(head_size)
    local_peak = jnp.max(scores, axis=2)
    peak_value = lax.pmax(local_peak, "seq")
    weights = jnp.exp(scores - peak_value[:, :, None])
    totals = jnp.sum(weights, axis=2)
    weighted = jnp.einsum(
        "qhk,khd->qhd",
        weights.astype(jnp.bfloat16),
        value_heads,
        preferred_element_type=jnp.float32,
    )
    totals, weighted = (totals, weighted.reshape(queries.shape[0], head_count * head_size))
    totals, weighted = (
        lax.psum_scatter(totals, "seq", scatter_dimension=0, tiled=True),
        lax.psum_scatter(weighted, "seq", scatter_dimension=0, tiled=True),
    )
    return (weighted / jnp.repeat(totals, head_size, axis=1)).astype(jnp.bfloat16)


def audio_block(audio_rows, audio_seen, norm_gain, up_weight, down_weight):
    features = lax.all_gather(audio_seen, "tp", axis=1, tiled=True)
    residual = audio_rows.astype(jnp.float32) + features.astype(jnp.float32)
    scale_factor = lax.rsqrt(jnp.mean(residual * residual, axis=1, keepdims=True) + 1e-06)
    normed = (residual * scale_factor * norm_gain).astype(jnp.bfloat16)
    slice_width = up_weight.shape[0]
    own_features = lax.dynamic_slice_in_dim(
        normed, lax.axis_index("tp") * slice_width, slice_width, 1
    )
    partial_sum = jnp.dot(
        lax.all_gather(own_features, "seq", axis=0, tiled=True),
        up_weight,
        preferred_element_type=jnp.float32,
    )
    hidden = jax.nn.gelu(lax.psum(partial_sum, "tp")).astype(jnp.bfloat16)
    return lax.psum_scatter(
        jnp.dot(hidden, down_weight, preferred_element_type=jnp.float32),
        "seq",
        scatter_dimension=0,
        tiled=True,
    ).astype(jnp.bfloat16)


def body(
    video_query,
    video_key,
    video_value,
    cross_query,
    audio_key,
    audio_value,
    audio_query,
    cross_key,
    cross_value,
    audio_input,
    norm_gain,
    up_weight,
    down_weight,
):
    if fits(lax.axis_size("seq"), video_query, audio_query, up_weight):
        args = (video_query, video_key, video_value, cross_query, audio_key, audio_value)
        args += (audio_query, cross_key, cross_value, audio_input)
        args = tuple(a[0] for a in args) + (norm_gain, up_weight, down_weight)
        outs = deliver(fused(lax.axis_size("seq"), lax.axis_size("tp"), args))
        return tuple(out[None] for out in outs)
    mixed_list, heard_list, seen_list, output_list = ([], [], [], [])
    cross_heads = cross_query.shape[2] // CHEAD
    mixed_list.append(video_self(video_query[0], video_key[0], video_value[0]))
    gathered_query = lax.all_gather(audio_query[0], "seq", axis=0, tiled=True)
    gathered_key = lax.all_gather(audio_key[0], "seq", axis=0, tiled=True)
    gathered_value = lax.all_gather(audio_value[0], "seq", axis=0, tiled=True)
    heard_list.append(attend(cross_query[0], gathered_key, gathered_value, cross_heads))
    audio_seen = audio_listen(gathered_query, cross_key[0], cross_value[0], cross_heads)
    seen_list.append(audio_seen)
    output_list.append(audio_block(audio_input[0], audio_seen, norm_gain, up_weight, down_weight))
    return (
        jnp.stack(mixed_list),
        jnp.stack(heard_list),
        jnp.stack(seen_list),
        jnp.stack(output_list),
    )


def solution(mesh):
    placed = (
        P(("clips", "dp"), "seq", "tp"),
        P(("clips", "dp"), "seq", "tp"),
        P(("clips", "dp"), "seq", "tp"),
        P(("clips", "dp"), "seq", "tp"),
        P(("clips", "dp"), "seq", "tp"),
        P(("clips", "dp"), "seq", "tp"),
        P(("clips", "dp"), "seq", "tp"),
        P(("clips", "dp"), "seq", "tp"),
        P(("clips", "dp"), "seq", "tp"),
        P(("clips", "dp"), "seq", None),
        P(),
        P("tp", "seq"),
        P("seq", "tp"),
    )
    return jax.shard_map(
        body,
        mesh=mesh,
        in_specs=placed,
        out_specs=(
            P(("clips", "dp"), "seq", "tp"),
            P(("clips", "dp"), "seq", "tp"),
            P(("clips", "dp"), "seq", "tp"),
            P(("clips", "dp"), "seq", "tp"),
        ),
        check_vma=False,
    )
```

```python
import functools
import math

import jax
import jax.numpy as jnp
from jax import lax
from jax.experimental import pallas as pl
from jax.experimental.pallas import tpu as pltpu
from jax.sharding import PartitionSpec as P

VHEAD = 128
CHEAD = 64
MESH = pl.DeviceIdType.MESH
LOG2E = math.log2(math.e)
CHUNKS = 4


def dot_t(a, b):
    return lax.dot_general(a, b, (((1,), (1,)), ((), ())), preferred_element_type=jnp.float32)


def softmax_parts(q, k, scale):
    s = dot_t(q, k)
    peak = jnp.max(s, axis=1, keepdims=True)
    p = jnp.exp2((s - peak) * (scale * LOG2E))
    return p, peak * scale, jnp.sum(p, axis=1, keepdims=True)


def pair_attend(q, k, v, scale):
    low = lax.broadcasted_iota(jnp.int32, q.shape, 1) < CHEAD
    zero = jnp.zeros_like(q)
    both = jnp.concatenate([jnp.where(low, q, zero), jnp.where(low, zero, q)], axis=0)
    p, peak, total = softmax_parts(both, k, scale)
    o = jnp.dot(p.astype(jnp.bfloat16), v, preferred_element_type=jnp.float32)
    return o, peak, total


def partners(me, n):
    if n & (n - 1):
        return [lax.rem(me + d, n) for d in range(1, n)]
    found = []
    for flip in range(n - 1, 0, -1):
        place, bit = me * 0, 1
        while bit < n:
            digit = lax.rem(lax.div(me, bit), 2)
            place = place + bit * ((1 - digit) if flip & bit else digit)
            bit *= 2
        found.append(place)
    return found


def fused_kernel(
    n, tp,
    vq, vk, vv, cq, ak, av, aq, ck, cv, ai, gain, up, down,
    mixed, heard, seen, mlp,
    qbuf, kbuf, vbuf, obuf, abuf, cqv, ckv, cvv, upv, downv, aiv, gainv, xsend, xrecv, tsend, trecv, hbuf, sbuf, mbuf, ssbuf, nbuf, pbuf, rsend, rrecv,
    v_send, v_recv, o_send, o_recv, a_send, a_recv, x_send, x_recv, t_send, t_recv, s_send, s_recv,
    n_send, n_recv, p_send, p_recv, r_send, r_recv, own_sem, oown_sem, load_sem,
):
    me = lax.axis_index("seq")
    col = lax.axis_index("tp")
    tokens = vq.shape[0]
    hd = vq.shape[1] // VHEAD // n
    rows, width = aq.shape
    pairs = width // 128
    units = up.shape[1]
    step = units // CHUNKS
    f32, bf16 = jnp.float32, jnp.bfloat16
    peers = partners(me, n)
    tp_peers = [lax.rem(col + d, tp) for d in range(1, tp)]

    def remote(src, dst, ss, rs, where):
        copy = pltpu.make_async_remote_copy(
            src_ref=src, dst_ref=dst, send_sem=ss, recv_sem=rs, device_id=where, device_id_type=MESH
        )
        copy.start()
        return copy

    barrier = pltpu.get_barrier_semaphore()
    for p in peers:
        pl.semaphore_signal(barrier, inc=1, device_id={"seq": p}, device_id_type=MESH)
    for t in tp_peers:
        pl.semaphore_signal(barrier, inc=1, device_id={"tp": t}, device_id_type=MESH)

    loads = []
    stays = ((ck, ckv), (cv, cvv), (cq, cqv), (up, upv), (down, downv), (ai, aiv), (gain, gainv))
    stays += tuple((src, abuf.at[i, me]) for i, src in enumerate((aq, ak, av)))
    for i, (src, dst) in enumerate(stays):
        loads.append(pltpu.make_async_copy(src, dst, load_sem.at[i]))
        loads[-1].start()
    owns = []
    for h in range(hd):
        cols = pl.ds(pl.multiple_of((me * hd + h) * VHEAD, VHEAD), VHEAD)
        owns.append([])
        for i, (src, buf) in enumerate(((vq, qbuf), (vk, kbuf), (vv, vbuf))):
            copy = pltpu.make_async_copy(src.at[:, cols], buf.at[h, me], own_sem.at[h, i])
            copy.start()
            owns[-1].append(copy)

    pl.semaphore_wait(barrier, n - 1 + tp - 1)

    sent = []

    def send_video(h):
        copies = []
        for d, p in enumerate(peers):
            cols = pl.ds(pl.multiple_of((p * hd + h) * VHEAD, VHEAD), VHEAD)
            for i, (src, buf) in enumerate(((vq, qbuf), (vk, kbuf), (vv, vbuf))):
                copies.append(
                    remote(src.at[:, cols], buf.at[h, me], v_send.at[h, d, i], v_recv.at[h, d, i], {"seq": p})
                )
        sent.extend(copies)
        return copies

    def attend_video(h, copies):
        for copy in owns[h]:
            copy.wait()
        for copy in copies:
            copy.wait_recv()
        k = kbuf[h].reshape(n * tokens, VHEAD)
        v = vbuf[h].reshape(n * tokens, VHEAD)
        cols = pl.ds(pl.multiple_of((me * hd + h) * VHEAD, VHEAD), VHEAD)
        out = []
        for d, p in enumerate(peers + [me]):
            w, _, total = softmax_parts(qbuf[h, p], k, 1.0 / math.sqrt(VHEAD))
            o = jnp.dot(w.astype(bf16), v, preferred_element_type=f32) / total
            obuf[h, p] = o.astype(bf16)
            if d < n - 1:
                out.append(remote(obuf.at[h, p], mixed.at[:, cols], o_send.at[h, d], o_recv.at[h, d], {"seq": p}))
        own = pltpu.make_async_copy(obuf.at[h, me], mixed.at[:, cols], oown_sem.at[h])
        own.start()
        return out, own

    relay = n == 4
    gathers, direct = [], []
    for i, src in enumerate((aq, ak, av)):
        for d, p in enumerate(peers):
            if i == 0 or not relay or d > 0:
                copy = remote(src, abuf.at[i, me], a_send.at[i, d], a_recv.at[i, d], {"seq": p})
                (direct if i else gathers).append(copy)
    sent.extend(gathers + direct)
    video = [send_video(0)]

    for copy in loads[:2] + loads[5:]:
        copy.wait()
    for copy in gathers:
        copy.wait_recv()

    def whole(i):
        return jnp.concatenate([abuf[i, s].astype(f32) for s in range(n)], axis=0).astype(bf16)

    scale = 1.0 / math.sqrt(CHEAD)
    total_rows = n * rows
    q_all = whole(0)
    lane = lax.broadcasted_iota(jnp.int32, (total_rows, 128), 1)
    stats = jnp.ones((total_rows, 128), f32)
    for j in range(pairs):
        at = slice(j * 128, (j + 1) * 128)
        o, peak, total = pair_attend(q_all[:, at], ckv[:, at], cvv[:, at], scale)
        picked = jnp.where(lane < CHEAD, o[:total_rows], o[total_rows:])
        xsend[:, :, at] = picked.reshape(n, rows, 128).astype(bf16)
        for half in range(2):
            part = slice(half * total_rows, (half + 1) * total_rows)
            stats = jnp.where(lane == 2 * j + half, peak[part], stats)
            stats = jnp.where(lane == 64 + 2 * j + half, total[part], stats)
    tsend[...] = stats.reshape(n, rows, 128)
    exchanges = []
    for d, p in enumerate(peers):
        exchanges.append(remote(tsend.at[p], trecv.at[me], t_send.at[d], t_recv.at[d], {"seq": p}))
        exchanges.append(remote(xsend.at[p], xrecv.at[me], x_send.at[d], x_recv.at[d], {"seq": p}))
    sent.extend(exchanges)
    xrecv[me] = xsend[me]
    trecv[me] = tsend[me]
    for h in range(1, min(2, hd)):
        video.append(send_video(h))

    loads[2].wait()
    for copy in direct:
        copy.wait_recv()
    if relay:
        passed = []
        for i in (1, 2):
            slot = abuf.at[i, peers[1]]
            passed.append(remote(slot, slot, a_send.at[i, 0], a_recv.at[i, 0], {"seq": peers[2]}))
        sent.extend(passed)
        for copy in passed:
            copy.wait_recv()
    k_all, v_all = whole(1), whole(2)
    wide = lax.broadcasted_iota(jnp.int32, (tokens, 128), 1)
    for j in range(pairs):
        at = slice(j * 128, (j + 1) * 128)
        o, _, total = pair_attend(cqv[:, at], k_all[:, at], v_all[:, at], scale)
        o = o / total
        hbuf[:, at] = jnp.where(wide < CHEAD, o[:tokens], o[tokens:]).astype(bf16)
    results_out = [pltpu.make_async_copy(hbuf, heard, load_sem.at[10])]
    results_out[-1].start()

    for copy in exchanges:
        copy.wait_recv()
    peak = trecv[0]
    for s in range(1, n):
        peak = jnp.maximum(peak, trecv[s])
    factors = [jnp.exp(trecv[s] - peak) for s in range(n)]
    total = sum(factors[s] * pltpu.roll(trecv[s], 64, 1) for s in range(n))
    factors = [f / total for f in factors]
    low = lax.broadcasted_iota(jnp.int32, (rows, 128), 1) < CHEAD
    pieces = []
    for j in range(pairs):
        at = slice(j * 128, (j + 1) * 128)
        value = jnp.zeros((rows, 128), f32)
        for s in range(n):
            f = factors[s]
            value += jnp.where(low, f[:, 2 * j : 2 * j + 1], f[:, 2 * j + 1 : 2 * j + 2]) * xrecv[s, :, at].astype(f32)
        pieces.append(value)
    seen_bf = jnp.concatenate(pieces, axis=1).astype(bf16)
    sbuf[...] = seen_bf
    results_out.append(pltpu.make_async_copy(sbuf, seen, load_sem.at[11]))
    results_out[-1].start()

    mine = pl.ds(pl.multiple_of(col * width, 128), width)
    residual = aiv[:, mine].astype(f32) + seen_bf.astype(f32)
    square = jnp.sum(residual * residual, axis=1, keepdims=True)
    ssbuf[col] = jnp.broadcast_to(square, (rows, 128))
    squares = []
    for d, t in enumerate(tp_peers):
        squares.append(remote(ssbuf.at[col], ssbuf.at[col], s_send.at[d], s_recv.at[d], {"tp": t}))
    sent.extend(squares)
    for copy in squares:
        copy.wait_recv()
    square = sum(ssbuf[t] for t in range(tp))[:, 0:1]
    factor = lax.rsqrt(square / (width * tp) + 1e-6)
    nbuf[me] = (residual * factor * gainv[:, mine]).astype(bf16)
    normed = []
    for d, p in enumerate(peers):
        normed.append(remote(nbuf.at[me], nbuf.at[me], n_send.at[d], n_recv.at[d], {"seq": p}))
    sent.extend(normed)
    for h in range(2, min(3, hd)):
        video.append(send_video(h))

    outs = [attend_video(0, video[0])]

    loads[3].wait()
    for copy in normed:
        copy.wait_recv()
    x = jnp.concatenate([nbuf[s].astype(f32) for s in range(n)], axis=0).astype(bf16)
    partials = []
    for c in range(CHUNKS):
        pbuf[col, c] = jnp.dot(x, upv[:, c * step : (c + 1) * step], preferred_element_type=f32)
        for d, t in enumerate(tp_peers):
            partials.append(
                remote(pbuf.at[col, c], pbuf.at[col, c], p_send.at[c, d], p_recv.at[c, d], {"tp": t})
            )
    sent.extend(partials)
    for h in range(3, hd):
        video.append(send_video(h))

    if hd > 1:
        outs.append(attend_video(1, video[1]))

    loads[4].wait()
    for copy in partials:
        copy.wait_recv()
    acc = jnp.zeros((total_rows, width), f32)
    for c in range(CHUNKS):
        hidden = jax.nn.gelu(sum(pbuf[t, c] for t in range(tp)), approximate=True).astype(bf16)
        acc += jnp.dot(hidden, downv[c * step : (c + 1) * step, :], preferred_element_type=f32)
    rsend[...] = acc.reshape(n, rows, width).astype(bf16)
    results = []
    for d, p in enumerate(peers):
        results.append(remote(rsend.at[p], rrecv.at[me], r_send.at[d], r_recv.at[d], {"seq": p}))
    sent.extend(results)
    rrecv[me] = rsend[me]

    for h in range(2, hd):
        outs.append(attend_video(h, video[h]))

    for copy in results:
        copy.wait_recv()
    mbuf[...] = sum(rrecv[s].astype(f32) for s in range(n)).astype(bf16)
    results_out.append(pltpu.make_async_copy(mbuf, mlp, load_sem.at[12]))
    results_out[-1].start()

    for out, own in outs:
        for copy in out:
            copy.wait()
        own.wait()
    for copy in results_out:
        copy.wait()
    for copy in sent:
        copy.wait_send()


def fused(n, tp, args):
    vq, vk, vv, cq, ak, av, aq, ck, cv, ai, gain, up, down = args
    tokens, vwidth = vq.shape
    hd = vwidth // VHEAD // n
    rows, width = aq.shape
    units = up.shape[1]
    bf16, f32 = jnp.bfloat16, jnp.float32
    anywhere = pl.BlockSpec(memory_space=pl.ANY)
    dma = pltpu.SemaphoreType.DMA
    head = pltpu.VMEM((hd, n, tokens, VHEAD), bf16)
    cross = pltpu.VMEM((tokens, width), bf16)
    z, t = max(n - 1, 1), max(tp - 1, 1)
    return pl.pallas_call(
        functools.partial(fused_kernel, n, tp),
        out_shape=(
            pltpu.VMEM((tokens, vwidth), bf16),
            pltpu.VMEM((tokens, width), bf16),
            pltpu.VMEM((rows, width), bf16),
            pltpu.VMEM((rows, width), bf16),
        ),
        in_specs=[anywhere] * 13,
        out_specs=(pl.BlockSpec(memory_space=pltpu.VMEM),) * 4,
        scratch_shapes=[
            head, head, head, head,
            pltpu.VMEM((3, n, rows, width), bf16),
            cross, cross, cross,
            pltpu.VMEM(up.shape, bf16),
            pltpu.VMEM(down.shape, bf16),
            pltpu.VMEM(ai.shape, bf16),
            pltpu.VMEM((1, gain.shape[0]), f32),
            pltpu.VMEM((n, rows, width), bf16),
            pltpu.VMEM((n, rows, width), bf16),
            pltpu.VMEM((n, rows, 128), f32),
            pltpu.VMEM((n, rows, 128), f32),
            cross,
            pltpu.VMEM((rows, width), bf16),
            pltpu.VMEM((rows, width), bf16),
            pltpu.VMEM((tp, rows, 128), f32),
            pltpu.VMEM((n, rows, width), bf16),
            pltpu.VMEM((tp, CHUNKS, n * rows, units // CHUNKS), f32),
            pltpu.VMEM((n, rows, width), bf16),
            pltpu.VMEM((n, rows, width), bf16),
            dma((hd, z, 3)), dma((hd, z, 3)), dma((hd, z)), dma((hd, z)),
            dma((3, z)), dma((3, z)), dma((z,)), dma((z,)), dma((z,)), dma((z,)), dma((t,)), dma((t,)),
            dma((z,)), dma((z,)), dma((CHUNKS, t)), dma((CHUNKS, t)), dma((z,)), dma((z,)),
            dma((hd, 3)), dma((hd,)), dma((13,)),
        ],
        compiler_params=pltpu.CompilerParams(collective_id=0, has_side_effects=True),
    )(vq, vk, vv, cq, ak, av, aq, ck, cv, ai, gain.reshape(1, -1), up, down)


def hand_over(*refs):
    count = (len(refs) - 1) // 2
    copies = [pltpu.make_async_copy(refs[i], refs[count + i], refs[-1].at[i]) for i in range(count)]
    for copy in copies:
        copy.start()
    for copy in copies:
        copy.wait()


def deliver(arrays):
    arrays = [pltpu.with_memory_space_constraint(a, pltpu.VMEM) for a in arrays]
    return pl.pallas_call(
        hand_over,
        out_shape=tuple(jax.ShapeDtypeStruct(a.shape, a.dtype) for a in arrays),
        in_specs=[pl.BlockSpec(memory_space=pltpu.VMEM)] * len(arrays),
        out_specs=(pl.BlockSpec(memory_space=pl.ANY),) * len(arrays),
        scratch_shapes=[pltpu.SemaphoreType.DMA((len(arrays),))],
    )(*arrays)


def fits(n, vq, aq, up):
    heads = vq.shape[2] // VHEAD
    return (
        heads % n == 0
        and vq.shape[1] % 16 == 0
        and aq.shape[1] % 8 == 0
        and aq.shape[2] % 128 == 0
        and aq.shape[2] // CHEAD <= 64
        and up.shape[0] == aq.shape[2]
        and up.shape[1] % (128 * CHUNKS) == 0
    )


def attend_rows(queries, keys_in, values_in, head_count):
    head_size = queries.shape[1] // head_count
    query_heads = queries.reshape(queries.shape[0], head_count, head_size)
    key_heads = keys_in.reshape(keys_in.shape[0], head_count, head_size)
    value_heads = values_in.reshape(values_in.shape[0], head_count, head_size)
    scores = jnp.einsum(
        "qhd,khd->qhk", query_heads, key_heads, preferred_element_type=jnp.float32
    ) / math.sqrt(head_size)
    peak_value = jnp.max(scores, axis=2, keepdims=True)
    weights = jnp.exp(scores - peak_value)
    totals = jnp.sum(weights, axis=2)
    weighted = jnp.einsum(
        "qhk,khd->qhd",
        weights.astype(jnp.bfloat16),
        value_heads,
        preferred_element_type=jnp.float32,
    )
    result = weighted / totals[:, :, None]
    return result.reshape(queries.shape[0], head_count * head_size).astype(jnp.bfloat16)


def attend(queries, keys_in, values_in, head_count):
    row_total = queries.shape[0]
    block_rows = 512 if row_total % 512 == 0 else row_total
    pieces = queries.reshape(row_total // block_rows, block_rows, queries.shape[1])
    result = lax.map(
        lambda row_piece: attend_rows(row_piece, keys_in, values_in, head_count), pieces
    )
    return result.reshape(row_total, queries.shape[1])


def video_self(queries, keys_in, values_in):
    seq_count = lax.axis_size("seq")
    local_heads = queries.shape[1] // VHEAD
    dest_heads = max(local_heads // seq_count, 1)
    blocks = seq_count * dest_heads // local_heads
    groups = local_heads // dest_heads
    group_width = dest_heads * VHEAD
    token_count = queries.shape[0]
    block_tokens = token_count // blocks

    def spread(tensor):
        shaped = tensor.reshape(token_count, groups, group_width).transpose(1, 0, 2)
        shaped = jnp.broadcast_to(shaped[:, None], (groups, blocks, token_count, group_width))
        return shaped.reshape(seq_count, token_count, group_width)

    shaped = queries.reshape(blocks, block_tokens, groups, group_width).transpose(2, 0, 1, 3)
    own_queries = lax.all_to_all(
        shaped.reshape(seq_count, block_tokens, group_width),
        "seq",
        split_axis=0,
        concat_axis=0,
        tiled=True,
    )
    keys_all = lax.all_to_all(spread(keys_in), "seq", split_axis=0, concat_axis=0, tiled=True)
    values_all = lax.all_to_all(spread(values_in), "seq", split_axis=0, concat_axis=0, tiled=True)
    keys_all = keys_all.reshape(-1, group_width)
    values_all = values_all.reshape(-1, group_width)
    own_queries = own_queries.reshape(-1, group_width)
    attended = attend(own_queries, keys_all, values_all, dest_heads)
    returned = lax.all_to_all(
        attended.reshape(seq_count, block_tokens, group_width),
        "seq",
        split_axis=0,
        concat_axis=0,
        tiled=True,
    )
    returned = returned.reshape(groups, blocks, block_tokens, group_width).transpose(1, 2, 0, 3)
    return returned.reshape(token_count, groups * group_width)


def audio_listen(queries, keys_in, values_in, head_count):
    head_size = queries.shape[1] // head_count
    query_heads = queries.reshape(queries.shape[0], head_count, head_size)
    key_heads = keys_in.reshape(keys_in.shape[0], head_count, head_size)
    value_heads = values_in.reshape(values_in.shape[0], head_count, head_size)
    scores = jnp.einsum(
        "qhd,khd->qhk", query_heads, key_heads, preferred_element_type=jnp.float32
    ) / math.sqrt(head_size)
    local_peak = jnp.max(scores, axis=2)
    peak_value = lax.pmax(local_peak, "seq")
    weights = jnp.exp(scores - peak_value[:, :, None])
    totals = jnp.sum(weights, axis=2)
    weighted = jnp.einsum(
        "qhk,khd->qhd",
        weights.astype(jnp.bfloat16),
        value_heads,
        preferred_element_type=jnp.float32,
    )
    totals, weighted = (totals, weighted.reshape(queries.shape[0], head_count * head_size))
    totals, weighted = (
        lax.psum_scatter(totals, "seq", scatter_dimension=0, tiled=True),
        lax.psum_scatter(weighted, "seq", scatter_dimension=0, tiled=True),
    )
    return (weighted / jnp.repeat(totals, head_size, axis=1)).astype(jnp.bfloat16)


def audio_block(audio_rows, audio_seen, norm_gain, up_weight, down_weight):
    features = lax.all_gather(audio_seen, "tp", axis=1, tiled=True)
    residual = audio_rows.astype(jnp.float32) + features.astype(jnp.float32)
    scale_factor = lax.rsqrt(jnp.mean(residual * residual, axis=1, keepdims=True) + 1e-06)
    normed = (residual * scale_factor * norm_gain).astype(jnp.bfloat16)
    slice_width = up_weight.shape[0]
    own_features = lax.dynamic_slice_in_dim(
        normed, lax.axis_index("tp") * slice_width, slice_width, 1
    )
    partial_sum = jnp.dot(
        lax.all_gather(own_features, "seq", axis=0, tiled=True),
        up_weight,
        preferred_element_type=jnp.float32,
    )
    hidden = jax.nn.gelu(lax.psum(partial_sum, "tp")).astype(jnp.bfloat16)
    return lax.psum_scatter(
        jnp.dot(hidden, down_weight, preferred_element_type=jnp.float32),
        "seq",
        scatter_dimension=0,
        tiled=True,
    ).astype(jnp.bfloat16)


def body(
    video_query,
    video_key,
    video_value,
    cross_query,
    audio_key,
    audio_value,
    audio_query,
    cross_key,
    cross_value,
    audio_input,
    norm_gain,
    up_weight,
    down_weight,
):
    if fits(lax.axis_size("seq"), video_query, audio_query, up_weight):
        args = (video_query, video_key, video_value, cross_query, audio_key, audio_value)
        args += (audio_query, cross_key, cross_value, audio_input)
        args = tuple(a[0] for a in args) + (norm_gain, up_weight, down_weight)
        outs = deliver(fused(lax.axis_size("seq"), lax.axis_size("tp"), args))
        return tuple(out[None] for out in outs)
    mixed_list, heard_list, seen_list, output_list = ([], [], [], [])
    cross_heads = cross_query.shape[2] // CHEAD
    mixed_list.append(video_self(video_query[0], video_key[0], video_value[0]))
    gathered_query = lax.all_gather(audio_query[0], "seq", axis=0, tiled=True)
    gathered_key = lax.all_gather(audio_key[0], "seq", axis=0, tiled=True)
    gathered_value = lax.all_gather(audio_value[0], "seq", axis=0, tiled=True)
    heard_list.append(attend(cross_query[0], gathered_key, gathered_value, cross_heads))
    audio_seen = audio_listen(gathered_query, cross_key[0], cross_value[0], cross_heads)
    seen_list.append(audio_seen)
    output_list.append(audio_block(audio_input[0], audio_seen, norm_gain, up_weight, down_weight))
    return (
        jnp.stack(mixed_list),
        jnp.stack(heard_list),
        jnp.stack(seen_list),
        jnp.stack(output_list),
    )


def solution(mesh):
    placed = (
        P(("clips", "dp"), "seq", "tp"),
        P(("clips", "dp"), "seq", "tp"),
        P(("clips", "dp"), "seq", "tp"),
        P(("clips", "dp"), "seq", "tp"),
        P(("clips", "dp"), "seq", "tp"),
        P(("clips", "dp"), "seq", "tp"),
        P(("clips", "dp"), "seq", "tp"),
        P(("clips", "dp"), "seq", "tp"),
        P(("clips", "dp"), "seq", "tp"),
        P(("clips", "dp"), "seq", None),
        P(),
        P("tp", "seq"),
        P("seq", "tp"),
    )
    return jax.shard_map(
        body,
        mesh=mesh,
        in_specs=placed,
        out_specs=(
            P(("clips", "dp"), "seq", "tp"),
            P(("clips", "dp"), "seq", "tp"),
            P(("clips", "dp"), "seq", "tp"),
            P(("clips", "dp"), "seq", "tp"),
        ),
        check_vma=False,
    )
```

```python
import functools
import math

import jax
import jax.numpy as jnp
from jax import lax
from jax.experimental import pallas as pl
from jax.experimental.pallas import tpu as pltpu
from jax.sharding import PartitionSpec as P

VHEAD = 128
CHEAD = 64
MESH = pl.DeviceIdType.MESH
LOG2E = math.log2(math.e)
CHUNKS = 4


def dot_t(a, b):
    return lax.dot_general(a, b, (((1,), (1,)), ((), ())), preferred_element_type=jnp.float32)


def softmax_parts(q, k, scale):
    s = dot_t(q, k)
    peak = jnp.max(s, axis=1, keepdims=True)
    p = jnp.exp2((s - peak) * (scale * LOG2E))
    return p, peak * scale, jnp.sum(p, axis=1, keepdims=True)


def pair_attend(q, k, v, scale):
    low = lax.broadcasted_iota(jnp.int32, q.shape, 1) < CHEAD
    zero = jnp.zeros_like(q)
    both = jnp.concatenate([jnp.where(low, q, zero), jnp.where(low, zero, q)], axis=0)
    p, peak, total = softmax_parts(both, k, scale)
    o = jnp.dot(p.astype(jnp.bfloat16), v, preferred_element_type=jnp.float32)
    return o, peak, total


def partners(me, n):
    if n & (n - 1):
        return [lax.rem(me + d, n) for d in range(1, n)]
    found = []
    for flip in range(n - 1, 0, -1):
        place, bit = me * 0, 1
        while bit < n:
            digit = lax.rem(lax.div(me, bit), 2)
            place = place + bit * ((1 - digit) if flip & bit else digit)
            bit *= 2
        found.append(place)
    return found


def fused_kernel(
    n, tp,
    vq, vk, vv, cq, ak, av, aq, ck, cv, ai, gain, up, down,
    mixed, heard, seen, mlp,
    qbuf, kbuf, vbuf, obuf, abuf, cqv, ckv, cvv, upv, downv, aiv, gainv, xsend, xrecv, tsend, trecv, hbuf, sbuf, mbuf, ssbuf, nbuf, pbuf, rsend, rrecv,
    v_send, v_recv, o_send, o_recv, a_send, a_recv, x_send, x_recv, t_send, t_recv, s_send, s_recv,
    n_send, n_recv, p_send, p_recv, r_send, r_recv, own_sem, oown_sem, load_sem,
):
    me = lax.axis_index("seq")
    col = lax.axis_index("tp")
    tokens = vq.shape[0]
    hd = vq.shape[1] // VHEAD // n
    rows, width = aq.shape
    pairs = width // 128
    units = up.shape[1]
    step = units // CHUNKS
    f32, bf16 = jnp.float32, jnp.bfloat16
    peers = partners(me, n)
    tp_peers = [lax.rem(col + d, tp) for d in range(1, tp)]

    def remote(src, dst, ss, rs, where):
        copy = pltpu.make_async_remote_copy(
            src_ref=src, dst_ref=dst, send_sem=ss, recv_sem=rs, device_id=where, device_id_type=MESH
        )
        copy.start()
        return copy

    barrier = pltpu.get_barrier_semaphore()
    for p in peers:
        pl.semaphore_signal(barrier, inc=1, device_id={"seq": p}, device_id_type=MESH)
    for t in tp_peers:
        pl.semaphore_signal(barrier, inc=1, device_id={"tp": t}, device_id_type=MESH)

    loads = []
    stays = ((ck, ckv), (cv, cvv), (cq, cqv), (up, upv), (down, downv), (ai, aiv), (gain, gainv))
    stays += tuple((src, abuf.at[i, me]) for i, src in enumerate((aq, ak, av)))
    for i, (src, dst) in enumerate(stays):
        loads.append(pltpu.make_async_copy(src, dst, load_sem.at[i]))
        loads[-1].start()
    owns = []
    for h in range(hd):
        cols = pl.ds(pl.multiple_of((me * hd + h) * VHEAD, VHEAD), VHEAD)
        owns.append([])
        for i, (src, buf) in enumerate(((vq, qbuf), (vk, kbuf), (vv, vbuf))):
            copy = pltpu.make_async_copy(src.at[:, cols], buf.at[h, me], own_sem.at[h, i])
            copy.start()
            owns[-1].append(copy)

    pl.semaphore_wait(barrier, n - 1 + tp - 1)

    sent = []

    def send_video(h):
        copies = []
        for d, p in enumerate(peers):
            cols = pl.ds(pl.multiple_of((p * hd + h) * VHEAD, VHEAD), VHEAD)
            for i, (src, buf) in enumerate(((vq, qbuf), (vk, kbuf), (vv, vbuf))):
                copies.append(
                    remote(src.at[:, cols], buf.at[h, me], v_send.at[h, d, i], v_recv.at[h, d, i], {"seq": p})
                )
        sent.extend(copies)
        return copies

    def attend_video(h, copies):
        for copy in owns[h]:
            copy.wait()
        for copy in copies:
            copy.wait_recv()
        k = kbuf[h].reshape(n * tokens, VHEAD)
        v = vbuf[h].reshape(n * tokens, VHEAD)
        cols = pl.ds(pl.multiple_of((me * hd + h) * VHEAD, VHEAD), VHEAD)
        out = []
        for d, p in enumerate(peers + [me]):
            w, _, total = softmax_parts(qbuf[h, p], k, 1.0 / math.sqrt(VHEAD))
            o = jnp.dot(w.astype(bf16), v, preferred_element_type=f32) / total
            obuf[h, p] = o.astype(bf16)
            if d < n - 1:
                out.append(remote(obuf.at[h, p], mixed.at[:, cols], o_send.at[h, d], o_recv.at[h, d], {"seq": p}))
        own = pltpu.make_async_copy(obuf.at[h, me], mixed.at[:, cols], oown_sem.at[h])
        own.start()
        return out, own

    relay = n == 4
    gathers, direct = [], []
    for i, src in enumerate((aq, ak, av)):
        for d, p in enumerate(peers):
            if i == 0 or not relay or d > 0:
                copy = remote(src, abuf.at[i, me], a_send.at[i, d], a_recv.at[i, d], {"seq": p})
                (direct if i else gathers).append(copy)
    sent.extend(gathers + direct)
    video = [send_video(0)]

    for copy in loads[:2] + loads[5:]:
        copy.wait()
    for copy in gathers:
        copy.wait_recv()

    def whole(i):
        return jnp.concatenate([abuf[i, s].astype(f32) for s in range(n)], axis=0).astype(bf16)

    scale = 1.0 / math.sqrt(CHEAD)
    total_rows = n * rows
    q_all = whole(0)
    lane = lax.broadcasted_iota(jnp.int32, (total_rows, 128), 1)
    stats = jnp.ones((total_rows, 128), f32)
    for j in range(pairs):
        at = slice(j * 128, (j + 1) * 128)
        o, peak, total = pair_attend(q_all[:, at], ckv[:, at], cvv[:, at], scale)
        picked = jnp.where(lane < CHEAD, o[:total_rows], o[total_rows:])
        xsend[:, :, at] = picked.reshape(n, rows, 128).astype(bf16)
        for half in range(2):
            part = slice(half * total_rows, (half + 1) * total_rows)
            stats = jnp.where(lane == 2 * j + half, peak[part], stats)
            stats = jnp.where(lane == 64 + 2 * j + half, total[part], stats)
    tsend[...] = stats.reshape(n, rows, 128)
    exchanges = []
    for d, p in enumerate(peers):
        exchanges.append(remote(tsend.at[p], trecv.at[me], t_send.at[d], t_recv.at[d], {"seq": p}))
        exchanges.append(remote(xsend.at[p], xrecv.at[me], x_send.at[d], x_recv.at[d], {"seq": p}))
    sent.extend(exchanges)
    xrecv[me] = xsend[me]
    trecv[me] = tsend[me]
    for h in range(1, min(2, hd)):
        video.append(send_video(h))

    loads[2].wait()
    for copy in direct:
        copy.wait_recv()
    if relay:
        passed = []
        for i in (1, 2):
            slot = abuf.at[i, peers[1]]
            passed.append(remote(slot, slot, a_send.at[i, 0], a_recv.at[i, 0], {"seq": peers[2]}))
        sent.extend(passed)
        for copy in passed:
            copy.wait_recv()
    k_all, v_all = whole(1), whole(2)
    wide = lax.broadcasted_iota(jnp.int32, (tokens, 128), 1)
    for j in range(pairs):
        at = slice(j * 128, (j + 1) * 128)
        o, _, total = pair_attend(cqv[:, at], k_all[:, at], v_all[:, at], scale)
        o = o / total
        hbuf[:, at] = jnp.where(wide < CHEAD, o[:tokens], o[tokens:]).astype(bf16)
    results_out = [pltpu.make_async_copy(hbuf, heard, load_sem.at[10])]
    results_out[-1].start()

    for copy in exchanges:
        copy.wait_recv()
    peak = trecv[0]
    for s in range(1, n):
        peak = jnp.maximum(peak, trecv[s])
    factors = [jnp.exp(trecv[s] - peak) for s in range(n)]
    total = sum(factors[s] * pltpu.roll(trecv[s], 64, 1) for s in range(n))
    factors = [f / total for f in factors]
    low = lax.broadcasted_iota(jnp.int32, (rows, 128), 1) < CHEAD
    pieces = []
    for j in range(pairs):
        at = slice(j * 128, (j + 1) * 128)
        value = jnp.zeros((rows, 128), f32)
        for s in range(n):
            f = factors[s]
            value += jnp.where(low, f[:, 2 * j : 2 * j + 1], f[:, 2 * j + 1 : 2 * j + 2]) * xrecv[s, :, at].astype(f32)
        pieces.append(value)
    seen_bf = jnp.concatenate(pieces, axis=1).astype(bf16)
    sbuf[...] = seen_bf
    results_out.append(pltpu.make_async_copy(sbuf, seen, load_sem.at[11]))
    results_out[-1].start()

    mine = pl.ds(pl.multiple_of(col * width, 128), width)
    residual = aiv[:, mine].astype(f32) + seen_bf.astype(f32)
    square = jnp.sum(residual * residual, axis=1, keepdims=True)
    ssbuf[col] = jnp.broadcast_to(square, (rows, 128))
    squares = []
    for d, t in enumerate(tp_peers):
        squares.append(remote(ssbuf.at[col], ssbuf.at[col], s_send.at[d], s_recv.at[d], {"tp": t}))
    sent.extend(squares)
    for copy in squares:
        copy.wait_recv()
    square = sum(ssbuf[t] for t in range(tp))[:, 0:1]
    factor = lax.rsqrt(square / (width * tp) + 1e-6)
    nbuf[me] = (residual * factor * gainv[:, mine]).astype(bf16)
    normed = []
    for d, p in enumerate(peers):
        if not relay or d > 0:
            normed.append(remote(nbuf.at[me], nbuf.at[me], n_send.at[d], n_recv.at[d], {"seq": p}))
    sent.extend(normed)
    for h in range(2, min(3, hd)):
        video.append(send_video(h))

    loads[3].wait()
    for copy in normed:
        copy.wait_recv()
    if relay:
        slot = nbuf.at[peers[1]]
        passed = remote(slot, slot, n_send.at[0], n_recv.at[0], {"seq": peers[2]})
        sent.append(passed)

    outs = [attend_video(0, video[0])]

    if relay:
        passed.wait_recv()
    x = jnp.concatenate([nbuf[s].astype(f32) for s in range(n)], axis=0).astype(bf16)
    partials = []
    for c in range(CHUNKS):
        pbuf[col, c] = jnp.dot(x, upv[:, c * step : (c + 1) * step], preferred_element_type=f32)
        for d, t in enumerate(tp_peers):
            partials.append(
                remote(pbuf.at[col, c], pbuf.at[col, c], p_send.at[c, d], p_recv.at[c, d], {"tp": t})
            )
    sent.extend(partials)
    for h in range(3, hd):
        video.append(send_video(h))

    if hd > 1:
        outs.append(attend_video(1, video[1]))

    loads[4].wait()
    for copy in partials:
        copy.wait_recv()
    acc = jnp.zeros((total_rows, width), f32)
    for c in range(CHUNKS):
        hidden = jax.nn.gelu(sum(pbuf[t, c] for t in range(tp)), approximate=True).astype(bf16)
        acc += jnp.dot(hidden, downv[c * step : (c + 1) * step, :], preferred_element_type=f32)
    rsend[...] = acc.reshape(n, rows, width).astype(bf16)
    results = []
    for d, p in enumerate(peers):
        results.append(remote(rsend.at[p], rrecv.at[me], r_send.at[d], r_recv.at[d], {"seq": p}))
    sent.extend(results)
    rrecv[me] = rsend[me]

    for h in range(2, hd):
        outs.append(attend_video(h, video[h]))

    for copy in results:
        copy.wait_recv()
    mbuf[...] = sum(rrecv[s].astype(f32) for s in range(n)).astype(bf16)
    results_out.append(pltpu.make_async_copy(mbuf, mlp, load_sem.at[12]))
    results_out[-1].start()

    for out, own in outs:
        for copy in out:
            copy.wait()
        own.wait()
    for copy in results_out:
        copy.wait()
    for copy in sent:
        copy.wait_send()


def fused(n, tp, args):
    vq, vk, vv, cq, ak, av, aq, ck, cv, ai, gain, up, down = args
    tokens, vwidth = vq.shape
    hd = vwidth // VHEAD // n
    rows, width = aq.shape
    units = up.shape[1]
    bf16, f32 = jnp.bfloat16, jnp.float32
    anywhere = pl.BlockSpec(memory_space=pl.ANY)
    dma = pltpu.SemaphoreType.DMA
    head = pltpu.VMEM((hd, n, tokens, VHEAD), bf16)
    cross = pltpu.VMEM((tokens, width), bf16)
    z, t = max(n - 1, 1), max(tp - 1, 1)
    return pl.pallas_call(
        functools.partial(fused_kernel, n, tp),
        out_shape=(
            pltpu.VMEM((tokens, vwidth), bf16),
            pltpu.VMEM((tokens, width), bf16),
            pltpu.VMEM((rows, width), bf16),
            pltpu.VMEM((rows, width), bf16),
        ),
        in_specs=[anywhere] * 13,
        out_specs=(pl.BlockSpec(memory_space=pltpu.VMEM),) * 4,
        scratch_shapes=[
            head, head, head, head,
            pltpu.VMEM((3, n, rows, width), bf16),
            cross, cross, cross,
            pltpu.VMEM(up.shape, bf16),
            pltpu.VMEM(down.shape, bf16),
            pltpu.VMEM(ai.shape, bf16),
            pltpu.VMEM((1, gain.shape[0]), f32),
            pltpu.VMEM((n, rows, width), bf16),
            pltpu.VMEM((n, rows, width), bf16),
            pltpu.VMEM((n, rows, 128), f32),
            pltpu.VMEM((n, rows, 128), f32),
            cross,
            pltpu.VMEM((rows, width), bf16),
            pltpu.VMEM((rows, width), bf16),
            pltpu.VMEM((tp, rows, 128), f32),
            pltpu.VMEM((n, rows, width), bf16),
            pltpu.VMEM((tp, CHUNKS, n * rows, units // CHUNKS), f32),
            pltpu.VMEM((n, rows, width), bf16),
            pltpu.VMEM((n, rows, width), bf16),
            dma((hd, z, 3)), dma((hd, z, 3)), dma((hd, z)), dma((hd, z)),
            dma((3, z)), dma((3, z)), dma((z,)), dma((z,)), dma((z,)), dma((z,)), dma((t,)), dma((t,)),
            dma((z,)), dma((z,)), dma((CHUNKS, t)), dma((CHUNKS, t)), dma((z,)), dma((z,)),
            dma((hd, 3)), dma((hd,)), dma((13,)),
        ],
        compiler_params=pltpu.CompilerParams(collective_id=0, has_side_effects=True),
    )(vq, vk, vv, cq, ak, av, aq, ck, cv, ai, gain.reshape(1, -1), up, down)


def hand_over(*refs):
    count = (len(refs) - 1) // 2
    copies = [pltpu.make_async_copy(refs[i], refs[count + i], refs[-1].at[i]) for i in range(count)]
    for copy in copies:
        copy.start()
    for copy in copies:
        copy.wait()


def deliver(arrays):
    arrays = [pltpu.with_memory_space_constraint(a, pltpu.VMEM) for a in arrays]
    return pl.pallas_call(
        hand_over,
        out_shape=tuple(jax.ShapeDtypeStruct(a.shape, a.dtype) for a in arrays),
        in_specs=[pl.BlockSpec(memory_space=pltpu.VMEM)] * len(arrays),
        out_specs=(pl.BlockSpec(memory_space=pl.ANY),) * len(arrays),
        scratch_shapes=[pltpu.SemaphoreType.DMA((len(arrays),))],
    )(*arrays)


def fits(n, vq, aq, up):
    heads = vq.shape[2] // VHEAD
    return (
        heads % n == 0
        and vq.shape[1] % 16 == 0
        and aq.shape[1] % 8 == 0
        and aq.shape[2] % 128 == 0
        and aq.shape[2] // CHEAD <= 64
        and up.shape[0] == aq.shape[2]
        and up.shape[1] % (128 * CHUNKS) == 0
    )


def attend_rows(queries, keys_in, values_in, head_count):
    head_size = queries.shape[1] // head_count
    query_heads = queries.reshape(queries.shape[0], head_count, head_size)
    key_heads = keys_in.reshape(keys_in.shape[0], head_count, head_size)
    value_heads = values_in.reshape(values_in.shape[0], head_count, head_size)
    scores = jnp.einsum(
        "qhd,khd->qhk", query_heads, key_heads, preferred_element_type=jnp.float32
    ) / math.sqrt(head_size)
    peak_value = jnp.max(scores, axis=2, keepdims=True)
    weights = jnp.exp(scores - peak_value)
    totals = jnp.sum(weights, axis=2)
    weighted = jnp.einsum(
        "qhk,khd->qhd",
        weights.astype(jnp.bfloat16),
        value_heads,
        preferred_element_type=jnp.float32,
    )
    result = weighted / totals[:, :, None]
    return result.reshape(queries.shape[0], head_count * head_size).astype(jnp.bfloat16)


def attend(queries, keys_in, values_in, head_count):
    row_total = queries.shape[0]
    block_rows = 512 if row_total % 512 == 0 else row_total
    pieces = queries.reshape(row_total // block_rows, block_rows, queries.shape[1])
    result = lax.map(
        lambda row_piece: attend_rows(row_piece, keys_in, values_in, head_count), pieces
    )
    return result.reshape(row_total, queries.shape[1])


def video_self(queries, keys_in, values_in):
    seq_count = lax.axis_size("seq")
    local_heads = queries.shape[1] // VHEAD
    dest_heads = max(local_heads // seq_count, 1)
    blocks = seq_count * dest_heads // local_heads
    groups = local_heads // dest_heads
    group_width = dest_heads * VHEAD
    token_count = queries.shape[0]
    block_tokens = token_count // blocks

    def spread(tensor):
        shaped = tensor.reshape(token_count, groups, group_width).transpose(1, 0, 2)
        shaped = jnp.broadcast_to(shaped[:, None], (groups, blocks, token_count, group_width))
        return shaped.reshape(seq_count, token_count, group_width)

    shaped = queries.reshape(blocks, block_tokens, groups, group_width).transpose(2, 0, 1, 3)
    own_queries = lax.all_to_all(
        shaped.reshape(seq_count, block_tokens, group_width),
        "seq",
        split_axis=0,
        concat_axis=0,
        tiled=True,
    )
    keys_all = lax.all_to_all(spread(keys_in), "seq", split_axis=0, concat_axis=0, tiled=True)
    values_all = lax.all_to_all(spread(values_in), "seq", split_axis=0, concat_axis=0, tiled=True)
    keys_all = keys_all.reshape(-1, group_width)
    values_all = values_all.reshape(-1, group_width)
    own_queries = own_queries.reshape(-1, group_width)
    attended = attend(own_queries, keys_all, values_all, dest_heads)
    returned = lax.all_to_all(
        attended.reshape(seq_count, block_tokens, group_width),
        "seq",
        split_axis=0,
        concat_axis=0,
        tiled=True,
    )
    returned = returned.reshape(groups, blocks, block_tokens, group_width).transpose(1, 2, 0, 3)
    return returned.reshape(token_count, groups * group_width)


def audio_listen(queries, keys_in, values_in, head_count):
    head_size = queries.shape[1] // head_count
    query_heads = queries.reshape(queries.shape[0], head_count, head_size)
    key_heads = keys_in.reshape(keys_in.shape[0], head_count, head_size)
    value_heads = values_in.reshape(values_in.shape[0], head_count, head_size)
    scores = jnp.einsum(
        "qhd,khd->qhk", query_heads, key_heads, preferred_element_type=jnp.float32
    ) / math.sqrt(head_size)
    local_peak = jnp.max(scores, axis=2)
    peak_value = lax.pmax(local_peak, "seq")
    weights = jnp.exp(scores - peak_value[:, :, None])
    totals = jnp.sum(weights, axis=2)
    weighted = jnp.einsum(
        "qhk,khd->qhd",
        weights.astype(jnp.bfloat16),
        value_heads,
        preferred_element_type=jnp.float32,
    )
    totals, weighted = (totals, weighted.reshape(queries.shape[0], head_count * head_size))
    totals, weighted = (
        lax.psum_scatter(totals, "seq", scatter_dimension=0, tiled=True),
        lax.psum_scatter(weighted, "seq", scatter_dimension=0, tiled=True),
    )
    return (weighted / jnp.repeat(totals, head_size, axis=1)).astype(jnp.bfloat16)


def audio_block(audio_rows, audio_seen, norm_gain, up_weight, down_weight):
    features = lax.all_gather(audio_seen, "tp", axis=1, tiled=True)
    residual = audio_rows.astype(jnp.float32) + features.astype(jnp.float32)
    scale_factor = lax.rsqrt(jnp.mean(residual * residual, axis=1, keepdims=True) + 1e-06)
    normed = (residual * scale_factor * norm_gain).astype(jnp.bfloat16)
    slice_width = up_weight.shape[0]
    own_features = lax.dynamic_slice_in_dim(
        normed, lax.axis_index("tp") * slice_width, slice_width, 1
    )
    partial_sum = jnp.dot(
        lax.all_gather(own_features, "seq", axis=0, tiled=True),
        up_weight,
        preferred_element_type=jnp.float32,
    )
    hidden = jax.nn.gelu(lax.psum(partial_sum, "tp")).astype(jnp.bfloat16)
    return lax.psum_scatter(
        jnp.dot(hidden, down_weight, preferred_element_type=jnp.float32),
        "seq",
        scatter_dimension=0,
        tiled=True,
    ).astype(jnp.bfloat16)


def body(
    video_query,
    video_key,
    video_value,
    cross_query,
    audio_key,
    audio_value,
    audio_query,
    cross_key,
    cross_value,
    audio_input,
    norm_gain,
    up_weight,
    down_weight,
):
    if fits(lax.axis_size("seq"), video_query, audio_query, up_weight):
        args = (video_query, video_key, video_value, cross_query, audio_key, audio_value)
        args += (audio_query, cross_key, cross_value, audio_input)
        args = tuple(a[0] for a in args) + (norm_gain, up_weight, down_weight)
        outs = deliver(fused(lax.axis_size("seq"), lax.axis_size("tp"), args))
        return tuple(out[None] for out in outs)
    mixed_list, heard_list, seen_list, output_list = ([], [], [], [])
    cross_heads = cross_query.shape[2] // CHEAD
    mixed_list.append(video_self(video_query[0], video_key[0], video_value[0]))
    gathered_query = lax.all_gather(audio_query[0], "seq", axis=0, tiled=True)
    gathered_key = lax.all_gather(audio_key[0], "seq", axis=0, tiled=True)
    gathered_value = lax.all_gather(audio_value[0], "seq", axis=0, tiled=True)
    heard_list.append(attend(cross_query[0], gathered_key, gathered_value, cross_heads))
    audio_seen = audio_listen(gathered_query, cross_key[0], cross_value[0], cross_heads)
    seen_list.append(audio_seen)
    output_list.append(audio_block(audio_input[0], audio_seen, norm_gain, up_weight, down_weight))
    return (
        jnp.stack(mixed_list),
        jnp.stack(heard_list),
        jnp.stack(seen_list),
        jnp.stack(output_list),
    )


def solution(mesh):
    placed = (
        P(("clips", "dp"), "seq", "tp"),
        P(("clips", "dp"), "seq", "tp"),
        P(("clips", "dp"), "seq", "tp"),
        P(("clips", "dp"), "seq", "tp"),
        P(("clips", "dp"), "seq", "tp"),
        P(("clips", "dp"), "seq", "tp"),
        P(("clips", "dp"), "seq", "tp"),
        P(("clips", "dp"), "seq", "tp"),
        P(("clips", "dp"), "seq", "tp"),
        P(("clips", "dp"), "seq", None),
        P(),
        P("tp", "seq"),
        P("seq", "tp"),
    )
    return jax.shard_map(
        body,
        mesh=mesh,
        in_specs=placed,
        out_specs=(
            P(("clips", "dp"), "seq", "tp"),
            P(("clips", "dp"), "seq", "tp"),
            P(("clips", "dp"), "seq", "tp"),
            P(("clips", "dp"), "seq", "tp"),
        ),
        check_vma=False,
    )
```
